128 devices in a mesh: tx: 16 (over x, y), ty: 8 (over z, core).
Axes of the slice: x: 4, y: 4, z: 4, core: 2. Of those that a mesh axis runs over, the one named last changes fastest.
Arguments:
- pressure: float32 [256, 128, 1], P('tx', 'ty'), may hold values from -6 to 6
- mobility: float32 [11, 256, 128, 1], P(None, 'tx', 'ty'), may hold values from 0.05 to 1
- mob_deriv: float32 [121, 256, 128, 1], P(None, 'tx', 'ty'), may hold values from -6 to 6
- accum: float32 [121, 256, 128, 1], P(None, 'tx', 'ty'), may hold values from -6 to 6
- trans: float32 [3, 256, 128, 1], P(None, 'tx', 'ty'), may hold values from 0.1 to 2
- upwind: int32 [3, 256, 128, 1], P(None, 'tx', 'ty'), may hold values 0 or 1
- fault_send: int32 [128, 128, 2], P(('tx', 'ty')), may hold values from 0 to 255
- fault_cell: int32 [128, 256], P(('tx', 'ty')), may hold values from 0 to 255, as said below
- fault_slot: int32 [128, 256], P(('tx', 'ty')), may hold values from 0 to 255, each once within a row
- fault_trans: float32 [128, 256], P(('tx', 'ty')), may hold values from 0.1 to 2
- fault_up: int32 [128, 256], P(('tx', 'ty')), may hold values 0 or 1
- cell_owner: int32 [32768, 1], P(('tx', 'ty')), may hold values from 0 to 127; in each aligned block of 256 rows (0 to 255, 256 to 511, ...) at most 4 rows name the same one
Outputs:
- relaid: bfloat16 [65536, 8, 256], P(('tx', 'ty'))
The draws below stay inside these ranges and needn't reach their ends.
Inputs may be any that keep to these rules, and one draw needn't show every extreme that they name: `fault_cell`: each tile's 256 entries are distinct local cells. `fault_slot`: each tile's row is a permutation of the received slots. `fault_send`: local cell indices of the sending tile. `cell_owner`: among the cells of one tile (aligned blocks of 256 in global cell order) at most 4 have the same owner.
All inputs are finite; a program needn't handle non-finite values. No bound on the sum of `upwind` or of `fault_up` on one device may be relied on, other than what follows from the above.
Results may differ from the reference program's by a relative error of at most 0.0045.
Values may be sent and summed in bfloat16 or wider, within the bound.
No kernel may reach another device: no remote copies, remote signals or barrier semaphores. Data moves between devices by JAX's collectives and lax.ppermute only.
A program may use at most 64 MiB of HBM per device.

```python
import math
import jax
import jax.numpy as jnp
import numpy as np

NEQ = 11
PAD = 16
GX = 16
GY = 16
NZ = 1
FCAP = 2
NDEV = 128
CELLS_DEV = 256
NFAULT = 256
CAPR = 4
NX = 256
NY = 128
CELLS = 32768
N_TX = 16
N_TY = 8


def draw_fault_cell(key, part):
    keys = jax.random.split(key, NDEV)
    picks = jax.vmap(lambda single: jax.random.permutation(single, CELLS_DEV)[:NFAULT])(keys)
    return picks.astype(jnp.int32)


def set_ends(entries, key, low, top_value):
    longest = entries.shape.index(max(entries.shape))
    spots = []
    for shift in (0, 1):
        where = [jax.random.randint(jax.random.fold_in(key, axis), (), 0, length) for axis, length in enumerate(entries.shape)]
        where[longest] = (where[longest] + shift) % entries.shape[longest]
        spots.append(tuple(where))
    return entries.at[spots[0]].set(low).at[spots[1]].set(top_value)


def level_of(own_key, shape, shards, smallest, high):
    loudness = 1.0
    for position, blocks in shards:
        steps = jax.random.uniform(jax.random.fold_in(jax.random.fold_in(own_key, 6), position), (blocks,), jnp.float32, smallest / len(shards), high / len(shards))
        loudness = loudness * jnp.repeat(jnp.exp(steps), shape[position] // blocks).reshape((-1,) + (1,) * (len(shape) - 1 - position))
    return loudness


def shared_out(stream_key, own, number, rows, amount, top, limit, skew):
    order = jax.random.permutation(stream_key, amount)
    heavy_load, usual = shares(amount, rows * top, limit, skew, True), shares(amount, rows * top, limit, skew, False)
    places = jnp.arange(amount)

    def named(tallies, turn):
        used = int((tallies > 0).sum())
        fixed = max(1, used // 4)
        shifted = fixed + (places - fixed + turn * (used - fixed)) % max(1, amount - fixed)
        return jnp.zeros((amount,), jnp.int32).at[order[jnp.where(places < fixed, places, shifted)]].set(jnp.asarray(tallies, jnp.int32))

    tallies = jnp.where(number % 4 == 0, named(heavy_load, number // 4), named(usual, number - number // 4 - 1))
    mixed = jax.random.permutation(jax.random.fold_in(own, 3), amount)
    giver, sink = mixed[0:amount // 2 * 2:2], mixed[1:amount // 2 * 2:2]
    margin = jnp.minimum(tallies[giver] - 1, limit - tallies[sink]) // 2
    margin = jnp.where((giver == order[0]) | (sink == order[0]) | (tallies[sink] == 0), 0, jnp.maximum(margin, 0))
    shifted = jax.random.randint(jax.random.fold_in(own, 4), (amount // 2,), 0, 1 << 20) % (margin + 1)
    tallies = tallies.at[giver].add(-shifted).at[sink].add(shifted)
    items = jnp.searchsorted(jnp.cumsum(tallies), jnp.arange(rows * top), side="right").astype(jnp.int32)
    table = items.reshape(top, rows).T
    table = table[jax.random.permutation(jax.random.fold_in(own, 1), rows)]
    turn = jax.random.randint(jax.random.fold_in(own, 2), (rows, 1), 0, top)
    return jnp.take_along_axis(table, (jnp.arange(top)[None, :] + turn) % top, axis=1)


def shares(count, total, limit, lean, full):
    weights = [(1 << 20) // math.isqrt(rank ** lean) + 1 for rank in range(1, count + 1)]
    largest = limit if full else min(limit, max(-(-total // count), total * weights[0] // sum(weights)))
    least = 1 if total - largest >= count - 1 else 0
    given, spare = [largest] + [least] * (count - 1), total - largest - least * (count - 1)
    while spare > 0:
        candidates = [i for i in range(1, count) if given[i] < largest] or [i for i in range(1, count) if given[i] < limit]
        whole, remaining = sum([weights[i] for i in candidates]), spare
        for i in candidates:
            extra = min(limit - given[i], max(1, remaining * weights[i] // whole), spare)
            given[i] = given[i] + extra
            spare = spare - extra
    return np.array(given)


def noise(own_key, extent, deviation, most, cuts=(), kind=jnp.bfloat16):
    values = deviation * jax.random.normal(own_key, extent, jnp.float32)
    if cuts:
        values = values * level_of(own_key, extent, cuts, -0.22, 0.18)
    return jnp.clip(values, -most, most).astype(kind)


def setup_inputs(seed: int = 0) -> dict:
    key_list = jax.random.split(jax.random.key(seed), 13)
    pressure = noise(key_list[0], (NX, NY, NZ), 1.0, 6.0, ((0, 16), (1, 8)), jnp.float32)
    mobility = jnp.clip(jnp.exp(math.log(1.0) - 2.9957323 * jax.random.uniform(key_list[1], (NEQ, NX, NY, NZ), jnp.float32) ** level_of(key_list[1], (NEQ, NX, NY, NZ), ((1, 16), (2, 8)), -0.2, 0.2)), 0.05, 1.0)
    mob_deriv = noise(key_list[2], (NEQ * NEQ, NX, NY, NZ), 1.0, 6.0, ((1, 16), (2, 8)), jnp.float32)
    accum = noise(key_list[3], (NEQ * NEQ, NX, NY, NZ), 1.0, 6.0, ((1, 16), (2, 8)), jnp.float32)
    trans = jnp.clip(jnp.exp(math.log(2.0) - 2.9957323 * jax.random.uniform(key_list[4], (3, NX, NY, NZ), jnp.float32) ** level_of(key_list[4], (3, NX, NY, NZ), ((1, 16), (2, 8)), -0.2, 0.2)), 0.1, 2.0)
    upwind = set_ends((jax.random.randint(key_list[5], (3, NX, NY, NZ), 0, 2) < 1).astype(jnp.int32), jax.random.fold_in(key_list[5], 1), 0, 1)
    fault_send = set_ends(jax.random.randint(key_list[6], (NDEV, NDEV, FCAP), 0, CELLS_DEV), jax.random.fold_in(key_list[6], 1), 0, CELLS_DEV - 1).astype(jnp.int32)
    fault_cell = draw_fault_cell(jax.random.fold_in(key_list[12], 71), 0)
    fault_slot = jax.vmap(lambda own: jax.random.permutation(own, NFAULT))(jax.random.split(key_list[8], NDEV)).reshape((NDEV, NFAULT)).astype(jnp.int32)
    fault_trans = jnp.clip(jnp.exp(math.log(2.0) - 2.9957323 * jax.random.uniform(key_list[9], (NDEV, NFAULT), jnp.float32) ** level_of(key_list[9], (NDEV, NFAULT), ((0, 128),), -0.2, 0.2)), 0.1, 2.0)
    fault_up = set_ends((jax.random.randint(key_list[10], (NDEV, NFAULT), 0, 2) < 1).astype(jnp.int32), jax.random.fold_in(key_list[10], 1), 0, 1)
    cell_owner_keys = jax.random.split(jax.random.fold_in(key_list[11], 1), CELLS // CELLS_DEV)
    cell_owner_turns = jax.random.permutation(jax.random.fold_in(key_list[11], 3), CELLS // CELLS_DEV)
    cell_owner = jax.vmap(lambda own, number: shared_out(jax.random.fold_in(key_list[11], 2), own, number, CELLS_DEV, NDEV, 1, CAPR, 4))(cell_owner_keys, cell_owner_turns).reshape((CELLS, 1))
    return {"pressure": pressure, "mobility": mobility, "mob_deriv": mob_deriv, "accum": accum, "trans": trans, "upwind": upwind, "fault_send": fault_send, "fault_cell": fault_cell, "fault_slot": fault_slot, "fault_trans": fault_trans, "fault_up": fault_up, "cell_owner": cell_owner}


def direction_terms(state_self, state_other, conduct, self_up, count):
    rest = state_self.shape[1:]
    lower = 1.0 - self_up
    diff = state_self[0] - state_other[0]
    mob_up = self_up * state_self[1:count + 1] + lower * state_other[1:count + 1]
    deriv_self = state_self[count + 1:].reshape((count, count) + rest)
    deriv_other = state_other[count + 1:].reshape((count, count) + rest)
    column = (jnp.arange(count) == 0).astype(jnp.float32).reshape((1, count) + (1,) * len(rest))
    pressure_part = mob_up[:, None] * column
    diag_part = conduct * (self_up * diff * deriv_self + pressure_part)
    off_part = conduct * (lower * diff * deriv_other - pressure_part)
    return diag_part, off_part


def to_devices(field):
    lead = field.shape[:-3]
    blocks = field.reshape(lead + (N_TX, GX, N_TY, GY, NZ))
    k = len(lead)
    order = tuple(range(k)) + (k, k + 2, k + 1, k + 3, k + 4)
    return jnp.transpose(blocks, order).reshape(lead + (NDEV, CELLS_DEV))


def reference(pressure, mobility, mob_deriv, accum, trans, upwind, fault_send, fault_cell, fault_slot, fault_trans, fault_up, cell_owner):
    count = NEQ
    nx, ny, nz = pressure.shape
    state = jnp.concatenate([pressure[None], mobility, mob_deriv], 0)
    flags = upwind.astype(jnp.float32)
    widen = ((0, 0), (1, 1), (1, 1), (1, 1))
    wide = jnp.pad(state, widen)
    trans_w = jnp.pad(trans, widen)
    flags_w = jnp.pad(flags, widen)

    def window(field, a, b, c):
        return field[:, a:a + nx, b:b + ny, c:c + nz]

    keep_x = (jnp.arange(nx) < nx - 1).astype(jnp.float32)[:, None, None]
    keep_y = (jnp.arange(ny) < ny - 1).astype(jnp.float32)[None, :, None]
    keep_z = (jnp.arange(nz) < nz - 1).astype(jnp.float32)[None, None, :]
    pairs = [
        (window(wide, 0, 1, 1), window(trans_w, 0, 1, 1)[0], 1.0 - window(flags_w, 0, 1, 1)[0]),
        (window(wide, 2, 1, 1), trans[0] * keep_x, flags[0]),
        (window(wide, 1, 0, 1), window(trans_w, 1, 0, 1)[1], 1.0 - window(flags_w, 1, 0, 1)[1]),
        (window(wide, 1, 2, 1), trans[1] * keep_y, flags[1]),
        (window(wide, 1, 1, 0), window(trans_w, 1, 1, 0)[2], 1.0 - window(flags_w, 1, 1, 0)[2]),
        (window(wide, 1, 1, 2), trans[2] * keep_z, flags[2]),
    ]
    diag = accum.reshape((count, count, nx, ny, nz))
    offs = []
    for other, conduct, self_up in pairs:
        diag_part, off_part = direction_terms(state, other, conduct, self_up, count)
        diag = diag + diag_part
        offs.append(to_devices(off_part))
    diag_dev = to_devices(diag)
    dev_state = to_devices(state)
    source = fault_slot // FCAP
    column = fault_slot % FCAP
    target = jnp.arange(NDEV, dtype=jnp.int32)[:, None] * jnp.ones_like(fault_slot)
    sent_cell = fault_send[source, target, column]
    partner = dev_state[:, source, sent_cell]
    mine = dev_state[:, target, fault_cell]
    fault_diag, fault_off = direction_terms(mine, partner, fault_trans, fault_up.astype(jnp.float32), count)
    diag_dev = diag_dev.at[:, :, target, fault_cell].add(fault_diag)
    fault_block = jnp.zeros((count, count, NDEV, CELLS_DEV), jnp.float32).at[:, :, target, fault_cell].set(fault_off)
    blocks = jnp.stack([diag_dev] + offs + [fault_block], 0).astype(jnp.bfloat16)
    blocks = jnp.pad(blocks, ((0, 0), (0, PAD - count), (0, PAD - count), (0, 0), (0, 0)))
    rows = jnp.transpose(blocks, (3, 4, 0, 1, 2)).reshape(NDEV * CELLS_DEV, 8, PAD * PAD)
    owner = cell_owner[:, 0].reshape(NDEV, CELLS_DEV)
    hits = (owner[:, :, None] == jnp.arange(NDEV, dtype=jnp.int32)[None, None, :]).astype(jnp.int32)
    rank = jnp.sum((jnp.cumsum(hits, 1) - hits) * hits, 2)
    sender = jnp.arange(NDEV, dtype=jnp.int32)[:, None]
    dest = owner * (NDEV * CAPR) + sender * CAPR + rank
    relaid = jnp.zeros((NDEV * NDEV * CAPR, 8, PAD * PAD), jnp.bfloat16).at[dest.reshape(-1)].set(rows)
    return relaid
```

```python
import functools

import jax
import jax.numpy as jnp
from jax import lax
from jax.experimental import pallas as pl
from jax.experimental.pallas import tpu as pltpu
from jax.sharding import PartitionSpec as P

PAD = 16
LANES = 128
BLOCKS = 8
SENT = 6
LOW = 32
F32 = jnp.float32
BF16 = jnp.bfloat16
EXACT = lax.Precision.HIGHEST


def iota(shape, dim):
    return lax.broadcasted_iota(jnp.int32, shape, dim)


def dot(a, b, contract=((1,), (0,)), precision=None):
    return lax.dot_general(
        a, b, (contract, ((), ())), precision=precision, preferred_element_type=F32
    )


NT = ((1,), (1,))


def lanes_of(count):
    return dict(p=0, m=1, tx=count + 1, ty=count + 2, ux=count + 3, uy=count + 4, here=count + 5)


def pack_kernel(p_ref, m_ref, t_ref, u_ref, l_ref, send_ref, c_ref, out_ref, xl_ref, xh_ref, yl_ref, yh_ref, ls_ref, ps_ref):
    wx, wy = p_ref.shape
    cells = wx * wy
    count = m_ref.shape[0]
    attrs = count + 5
    up = u_ref[0:2].astype(F32)
    field = jnp.concatenate([p_ref[...][None], m_ref[...], t_ref[0:2], up], 0)
    field = field.reshape(attrs * wx, wy)
    pick_y = ((iota((cells, wy), 0) & (wy - 1)) == iota((cells, wy), 1)).astype(F32)
    spread = dot(pick_y, field, NT, EXACT)
    own_x = (iota(spread.shape, 1) & (wx - 1)) == (iota(spread.shape, 0) // wy)
    spread = jnp.where(own_x, spread, 0.0)
    fold = ((iota((attrs * wx, LANES), 0) // wx) == iota((attrs * wx, LANES), 1)).astype(F32)
    scal = dot(spread, fold, ((1,), (0,)), EXACT)
    scal = jnp.where(iota(scal.shape, 1) == lanes_of(count)["here"], 1.0, scal)
    c_ref[...] = scal
    high = scal.astype(BF16).astype(F32)
    ps_ref[...] = high + pltpu.roll(scal - high, LOW, 1)
    ls_ref[...] = jnp.zeros_like(ls_ref)
    ls_ref[:, 0 : l_ref.shape[1]] = l_ref[...]

    def edge(ref, rows):
        ref[0:wx, :] = ls_ref[rows, :].astype(BF16)
        ref[wx : 2 * wx, :] = ps_ref[rows, :].astype(BF16)

    edge(xl_ref, pl.ds(0, wy))
    edge(xh_ref, pl.ds(cells - wy, wy))
    edge(yl_ref, pl.ds(0, wx, stride=wy))
    edge(yh_ref, pl.ds(wy - 1, wx, stride=wy))

    devices = send_ref.shape[1]
    rows = out_ref.shape[0]
    send = jnp.concatenate([send_ref[...], jnp.zeros((6, devices), jnp.int32)], 0).astype(F32)
    pick_d = ((iota((rows, devices), 0) >> 2) == iota((rows, devices), 1)).astype(BF16)
    picks = dot(pick_d, send.astype(BF16), NT)
    odd = (iota((rows, 1), 0) & 1) == 1
    picks = jnp.where(odd, picks[:, 1:2], picks[:, 0:1]).astype(jnp.int32)
    picks = picks + ((iota((rows, 1), 0) >> 1) & 1) * cells
    onehot = (iota((rows, 2 * cells), 1) == picks).astype(F32).astype(BF16)
    both = jnp.concatenate([ls_ref[...], ps_ref[...]], 0).astype(BF16)
    out_ref[...] = dot(onehot, both).astype(BF16)


def rows_kernel(c_ref, l_ref, a_ref, xl_ref, xh_ref, yl_ref, yh_ref, arr_ref, cell_ref, slot_ref, ft_ref, fu_ref, own_ref, out_ref, ls_ref):
    cells = c_ref.shape[0]
    wx = xl_ref.shape[0] // 2
    wy = cells // wx
    width = l_ref.shape[1]
    devices = out_ref.shape[0]
    count = 1
    while count * count < width:
        count += 1
    lane = lanes_of(count)
    scal = c_ref[...]
    ls_ref[...] = jnp.zeros_like(ls_ref)
    ls_ref[:, 0:width] = l_ref[...]
    deriv = ls_ref[...]
    ls_ref[:, 0:width] = a_ref[...]
    accum = ls_ref[...]

    def unpack(both):
        half = both.shape[0] // 2
        low = both[half:]
        return both[0:half], low + pltpu.roll(low, LANES - LOW, 1)

    def repeat(edge):
        return jnp.broadcast_to(edge[:, None, :], (wx, wy, LANES)).reshape(cells, LANES)

    at_y = iota((cells, 1), 0) & (wy - 1)
    xl_l, xl_c = unpack(xl_ref[...].astype(F32))
    xh_l, xh_c = unpack(xh_ref[...].astype(F32))
    yl_l, yl_c = unpack(yl_ref[...].astype(F32))
    yh_l, yh_c = unpack(yh_ref[...].astype(F32))

    def left(body, edge):
        return jnp.concatenate([edge, body[0 : cells - wy]], 0)

    def right(body, edge):
        return jnp.concatenate([body[wy:], edge], 0)

    def below(body, edge):
        return jnp.where(at_y == 0, repeat(edge), pltpu.roll(body, 1, 0))

    def above(body, edge):
        return jnp.where(at_y == wy - 1, repeat(edge), pltpu.roll(body, cells - 1, 0))

    def col(value, name):
        return value[:, lane[name] : lane[name] + 1]

    kcell = (iota((cells, cells), 0) == cell_ref[...]).astype(F32)
    info = jnp.concatenate(
        [slot_ref[...].astype(F32), ft_ref[...], fu_ref[...].astype(F32), jnp.zeros((5, cells), F32)], 0
    )
    info = dot(kcell, info, NT, EXACT)
    slot = info[:, 0:1].astype(jnp.int32)
    place = (slot >> 1) * 4 + (slot & 1)
    place = jnp.concatenate([place, place + 2], 0)
    pick = (iota((2 * cells, arr_ref.shape[0]), 1) == place).astype(F32).astype(BF16)
    far_l, far_c = unpack(dot(pick, arr_ref[...]))

    moved = []
    scale = jnp.zeros((cells, 1), F32)
    columns = []

    def connect(other_l, other_c, t, w):
        nonlocal scale
        drop = t * (col(scal, "p") - col(other_c, "p"))
        scale = scale + w * drop
        moved.append(((1.0 - w) * drop) * other_l)
        columns.append((t * w) * scal + (t * (1.0 - w)) * other_c)

    other = left(scal, xl_c)
    connect(left(deriv, xl_l), other, col(other, "tx"), 1.0 - col(other, "ux"))
    other = right(scal, xh_c)
    connect(right(deriv, xh_l), other, col(scal, "tx") * col(other, "here"), col(scal, "ux"))
    other = below(scal, yl_c)
    connect(below(deriv, yl_l), other, col(other, "ty"), 1.0 - col(other, "uy"))
    other = above(scal, yh_c)
    connect(above(deriv, yh_l), other, col(scal, "ty") * col(other, "here"), col(scal, "uy"))
    connect(far_l, far_c, info[:, 1:2], info[:, 2:3])

    to = iota((LANES, LANES), 1)
    src = iota((LANES, LANES), 0)
    first = ((src >= 1) & (src <= count) & (to == (src - 1) * count)).astype(F32)
    spread = dot(jnp.concatenate(columns, 0), first, ((1,), (0,)), EXACT)
    parts = [spread[i * cells : (i + 1) * cells] for i in range(5)]
    total = parts[0] + parts[1] + parts[2] + parts[3] + parts[4]
    blocks = [accum + scale * deriv + total] + [m - c for m, c in zip(moved, parts)]
    blocks = [block.astype(BF16) for block in blocks]
    pairs = [jnp.concatenate(blocks[i : i + 2], 0) for i in range(0, SENT, 2)]
    stacked = jnp.concatenate(pairs, 1)

    owner = own_ref[...]
    hits = (iota((devices, cells), 0) == owner).astype(F32)
    before = (iota((cells, cells), 0) < iota((cells, cells), 1)).astype(BF16)
    earlier = dot(hits.astype(BF16), before)
    rank = jnp.sum(earlier * hits, 0, keepdims=True)
    target = owner * 4 + rank.astype(jnp.int32)
    row = iota((devices * 8, cells), 0)
    match = ((row >> 3) * 4 + (row & 3)) == target
    odd = (row & 4) == 4
    placement = jnp.concatenate(
        [jnp.where(match & ~odd, 1.0, 0.0).astype(BF16), jnp.where(match & odd, 1.0, 0.0).astype(BF16)], 1
    )
    placed = dot(placement, stacked)
    for i in range(SENT // 2):
        part = placed[:, i * LANES : (i + 1) * LANES]
        out_ref[:, i * 8 : (i + 1) * 8, :] = part.reshape(devices, 8, LANES).astype(BF16)


def expand_kernel(count, in_ref, out_ref, order_ref, widen_ref):
    tall, deep = order_ref.shape
    wide = widen_ref.shape[1]

    @pl.when(pl.program_id(0) == 0)
    def _():
        o = iota((tall, deep), 0)
        i = iota((tall, deep), 1)
        block = o & 7
        kept = jnp.where(block == 7, 5, block)
        want = (o >> 5) * (SENT * 4) + kept * 4 + ((o >> 3) & 3)
        keep = (block != 5) & (block != 6) & (i == want)
        order_ref[...] = jnp.where(keep, 1.0, 0.0).astype(BF16)
        src = iota((LANES, wide), 0)
        to = iota((LANES, wide), 1)
        r, c = to // PAD, to % PAD
        keep = (r < count) & (c < count) & (src == r * count + c)
        widen_ref[...] = jnp.where(keep, 1.0, 0.0).astype(BF16)

    groups = in_ref.shape[0] // deep
    for g in range(groups):
        rows = dot(order_ref[...], in_ref[g * deep : (g + 1) * deep, :]).astype(BF16)
        full = dot(rows, widen_ref[...])
        per = tall // BLOCKS
        out_ref[g * per : (g + 1) * per] = full.reshape(per, BLOCKS, wide).astype(BF16)


def body(pressure, mobility, mob_deriv, accum, trans, upwind, fault_send, fault_cell, fault_slot, fault_trans, fault_up, cell_owner):
    wx, wy, _ = pressure.shape
    count = mobility.shape[0]
    cells = wx * wy
    nx, ny = lax.axis_size("tx"), lax.axis_size("ty")
    devices = nx * ny
    deriv = jnp.transpose(mob_deriv, (1, 2, 3, 0)).reshape(cells, count * count)
    accumulated = jnp.transpose(accum, (1, 2, 3, 0)).reshape(cells, count * count)
    edge = jax.ShapeDtypeStruct((2 * wx, LANES), BF16)
    scal, outgoing, xl, xh, yl, yh = pl.pallas_call(
        pack_kernel,
        out_shape=(
            jax.ShapeDtypeStruct((cells, LANES), F32),
            jax.ShapeDtypeStruct((devices * 4, LANES), BF16),
            edge,
            edge,
            edge,
            edge,
        ),
        scratch_shapes=[pltpu.VMEM((cells, LANES), F32), pltpu.VMEM((cells, LANES), F32)],
        name="pack",
    )(pressure[..., 0], mobility[..., 0], trans[..., 0], upwind[..., 0], deriv, fault_send[0].T)
    up_x = [(i, i + 1) for i in range(nx - 1)]
    up_y = [(i, i + 1) for i in range(ny - 1)]
    from_xl = lax.ppermute(xh, "tx", up_x)
    from_xh = lax.ppermute(xl, "tx", [(b, a) for a, b in up_x])
    from_yl = lax.ppermute(yh, "ty", up_y)
    from_yh = lax.ppermute(yl, "ty", [(b, a) for a, b in up_y])
    arrived = lax.all_to_all(
        outgoing.reshape(devices, 4, LANES), ("tx", "ty"), split_axis=0, concat_axis=0, tiled=True
    ).reshape(devices * 4, LANES)
    buffer = pl.pallas_call(
        rows_kernel,
        out_shape=jax.ShapeDtypeStruct((devices, SENT * 4, LANES), BF16),
        scratch_shapes=[pltpu.VMEM((cells, LANES), F32)],
        compiler_params=pltpu.CompilerParams(vmem_limit_bytes=40 << 20),
        name="rows",
    )(
        scal, deriv, accumulated, from_xl, from_xh, from_yl, from_yh, arrived,
        fault_cell, fault_slot, fault_trans, fault_up, cell_owner.reshape(1, cells),
    )
    landed = lax.all_to_all(buffer, ("tx", "ty"), split_axis=0, concat_axis=0, tiled=True)
    landed = landed.reshape(devices * SENT * 4, LANES)
    steps = 4
    per = devices // steps
    group = 8
    return pl.pallas_call(
        functools.partial(expand_kernel, count),
        out_shape=jax.ShapeDtypeStruct((devices * 4, BLOCKS, PAD * PAD), BF16),
        grid=(steps,),
        in_specs=[pl.BlockSpec((per * SENT * 4, LANES), lambda i: (i, 0))],
        out_specs=pl.BlockSpec((per * 4, BLOCKS, PAD * PAD), lambda i: (i, 0, 0)),
        scratch_shapes=[
            pltpu.VMEM((group * 4 * BLOCKS, group * SENT * 4), BF16),
            pltpu.VMEM((LANES, PAD * PAD), BF16),
        ],
        name="expand",
    )(landed)


def solution(mesh):
    in_specs = (
        P("tx", "ty", None),
        P(None, "tx", "ty", None),
        P(None, "tx", "ty", None),
        P(None, "tx", "ty", None),
        P(None, "tx", "ty", None),
        P(None, "tx", "ty", None),
        P(("tx", "ty"), None, None),
        P(("tx", "ty"), None),
        P(("tx", "ty"), None),
        P(("tx", "ty"), None),
        P(("tx", "ty"), None),
        P(("tx", "ty"), None),
    )
    out_specs = P(("tx", "ty"), None, None)
    return jax.shard_map(body, mesh=mesh, in_specs=in_specs, out_specs=out_specs, check_vma=False)
```

```python
import functools

import jax
import jax.numpy as jnp
from jax import lax
from jax.experimental import pallas as pl
from jax.experimental.pallas import tpu as pltpu
from jax.sharding import PartitionSpec as P

PAD = 16
LANES = 128
BLOCKS = 8
SENT = 6
HALF = 16
SLOT = 32
F32 = jnp.float32
BF16 = jnp.bfloat16
EXACT = lax.Precision.HIGHEST


def iota(shape, dim):
    return lax.broadcasted_iota(jnp.int32, shape, dim)


def dot(a, b, contract=((1,), (0,)), precision=None):
    return lax.dot_general(
        a, b, (contract, ((), ())), precision=precision, preferred_element_type=F32
    )


NT = ((1,), (1,))


def lanes_of(count):
    return dict(p=0, m=1, tx=count + 1, ty=count + 2, ux=count + 3, uy=count + 4, here=count + 5)


def neighbours(nx, ny):
    ix, iy = lax.axis_index("tx"), lax.axis_index("ty")
    me = ix * ny + iy
    there = [ix > 0, ix < nx - 1, iy > 0, iy < ny - 1]
    return [(jnp.where(ok, me + step, me), ok) for ok, step in zip(there, (-ny, ny, -1, 1))]


def pack_kernel(nx, ny, p_ref, m_ref, t_ref, u_ref, l_ref, send_ref, c_ref, out_ref, ls_ref, ps_ref):
    wx, wy = p_ref.shape
    cells = wx * wy
    count = m_ref.shape[0]
    attrs = count + 5
    up = u_ref[0:2].astype(F32)
    field = jnp.concatenate([p_ref[...][None], m_ref[...], t_ref[0:2], up], 0)
    field = field.reshape(attrs * wx, wy)
    pick_y = ((iota((cells, wy), 0) & (wy - 1)) == iota((cells, wy), 1)).astype(F32)
    spread = dot(pick_y, field, NT, EXACT)
    own_x = (iota(spread.shape, 1) & (wx - 1)) == (iota(spread.shape, 0) // wy)
    spread = jnp.where(own_x, spread, 0.0)
    fold = ((iota((attrs * wx, LANES), 0) // wx) == iota((attrs * wx, LANES), 1)).astype(F32)
    scal = dot(spread, fold, ((1,), (0,)), EXACT)
    scal = jnp.where(iota(scal.shape, 1) == lanes_of(count)["here"], 1.0, scal)
    c_ref[...] = scal
    high = scal.astype(BF16).astype(F32)
    ps_ref[...] = jnp.where(iota(scal.shape, 1) < HALF, high, 0.0) + pltpu.roll(scal - high, HALF, 1)
    ls_ref[...] = jnp.zeros_like(ls_ref)
    ls_ref[:, 0 : l_ref.shape[1]] = l_ref[...]

    devices = send_ref.shape[1]
    rows = devices * 8
    send = jnp.concatenate([send_ref[...], jnp.zeros((6, devices), jnp.int32)], 0).astype(F32)
    pick_d = ((iota((rows, devices), 0) >> 3) == iota((rows, devices), 1)).astype(BF16)
    picks = dot(pick_d, send.astype(BF16), NT)
    row = iota((rows, 1), 0)
    picks = jnp.where((row & 1) == 1, picks[:, 1:2], picks[:, 0:1]).astype(jnp.int32)
    picks = jnp.where((row & 4) == 4, -1, picks + ((row >> 1) & 1) * cells)
    onehot = (iota((rows, 2 * cells), 1) == picks).astype(F32).astype(BF16)
    both = jnp.concatenate([ls_ref[...], ps_ref[...]], 0).astype(BF16)
    side = out_ref.shape[1] - 8
    out_ref[:, 0:side, :] = jnp.zeros((devices, side, LANES), BF16)
    far = dot(onehot, both)
    out_ref[:, side:, :] = far.reshape(devices, 8, LANES).astype(BF16)

    edges = [pl.ds(0, wy), pl.ds(cells - wy, wy), pl.ds(0, wx, stride=wy), pl.ds(wy - 1, wx, stride=wy)]
    sides = jnp.concatenate([ps_ref[rows_of, :] for rows_of in edges], 0).astype(BF16)
    tiles = dot(gather_tiles(side), jnp.where(own_lanes(4 * side), dot(sides, repeat_lanes()), 0.0).astype(BF16))
    for i, (device, there) in enumerate(neighbours(nx, ny)):

        @pl.when(there)
        def _():
            out_ref[device, 0:side, :] = ls_ref[edges[i], :].astype(BF16)
            old = out_ref[device, side : side + 8, :].astype(F32)
            out_ref[device, side : side + 8, :] = (old + tiles[i * 8 : (i + 1) * 8]).astype(BF16)


def repeat_lanes():
    return ((iota((LANES, LANES), 1) & (SLOT - 1)) == iota((LANES, LANES), 0)).astype(F32).astype(BF16)


def own_lanes(rows):
    return (iota((rows, LANES), 1) // SLOT) == (iota((rows, LANES), 0) & 3)


def gather_tiles(side):
    shape = (4 * 8, 4 * side)
    tile, cell = iota(shape, 0), iota(shape, 1)
    keep = ((tile >> 3) == cell // side) & ((tile & 7) == 4 + ((cell & (side - 1)) >> 2))
    return keep.astype(F32).astype(BF16)


def spread_matrix(count):
    src, to = iota((LANES, LANES), 0), iota((LANES, LANES), 1)
    keep = (src >= 1) & (src <= count) & (to == (src - 1) * count)
    return keep.astype(F32).astype(BF16)


def spread(columns, matrix):
    high = columns.astype(BF16)
    low = (columns - high.astype(F32)).astype(BF16)
    return dot(high, matrix) + dot(low, matrix)


def coupling(scal, deriv, other_l, other_c, t, w):
    drop = t * (scal[:, 0:1] - other_c[:, 0:1])
    columns = (t * w) * scal + (t * (1.0 - w)) * other_c
    return w * drop, ((1.0 - w) * drop) * other_l, columns


def local_kernel(count, devices, wx, wy, c_ref, l_ref, a_ref, cell_ref, slot_ref, ft_ref, fu_ref, own_ref, base_ref, info_ref, pick_ref, put_ref, ls_ref):
    cells, width = l_ref.shape
    lane = lanes_of(count)
    scal = c_ref[...]
    ls_ref[...] = jnp.zeros_like(ls_ref)
    ls_ref[:, 0:width] = a_ref[...]
    accum = ls_ref[...]
    ls_ref[:, 0:width] = l_ref[...]
    deriv = ls_ref[...]
    at = iota((cells, 1), 0)
    at_x, at_y = at // wy, at & (wy - 1)
    first = spread_matrix(count)

    def col(value, name):
        return value[:, lane[name] : lane[name] + 1]

    scale = jnp.zeros((cells, 1), F32)
    total = jnp.zeros((cells, LANES), F32)
    steps = [(wy, "tx", "ux", at_x == 0), (cells - wy, "tx", "ux", at_x == wx - 1), (1, "ty", "uy", at_y == 0), (cells - 1, "ty", "uy", at_y == wy - 1)]
    for i, (step, trans, up, rim) in enumerate(steps):
        other_c, other_l = pltpu.roll(scal, step, 0), pltpu.roll(deriv, step, 0)
        if i % 2 == 0:
            t, w = col(other_c, trans), 1.0 - col(other_c, up)
        else:
            t, w = col(scal, trans), col(scal, up)
        t = jnp.where(rim, 0.0, t)
        share, moved, columns = coupling(scal, deriv, other_l, other_c, t, w)
        part = spread(columns, first)
        scale = scale + share
        total = total + part
        base_ref[(i + 1) * cells : (i + 2) * cells, :] = moved - part
    base_ref[0:cells, :] = accum + scale * deriv + total
    base_ref[5 * cells : 6 * cells, :] = deriv

    kcell = (iota((cells, cells), 0) == cell_ref[...]).astype(F32)
    info = jnp.concatenate(
        [slot_ref[...].astype(F32), ft_ref[...], fu_ref[...].astype(F32), jnp.zeros((5, cells), F32)], 0
    )
    info = dot(kcell, info, NT, EXACT)
    info_ref[...] = info
    slot = info[:, 0:1].astype(jnp.int32)
    place = (slot >> 1) * 8 + (slot & 1)
    place = jnp.concatenate([place, place + 2], 0)
    pick_ref[...] = (iota((2 * cells, devices * 8), 1) == place).astype(F32).astype(BF16)

    owner = own_ref[...]
    hits = (iota((devices, cells), 0) == owner).astype(F32)
    before = (iota((cells, cells), 0) < iota((cells, cells), 1)).astype(F32).astype(BF16)
    earlier = dot(hits.astype(BF16), before)
    rank = jnp.sum(earlier * hits, 0, keepdims=True)
    target = owner * 4 + rank.astype(jnp.int32)
    row = iota((devices * 8, cells), 0)
    match = ((row >> 3) * 4 + (row & 3)) == target
    odd = (row & 4) == 4
    put_ref[:, 0:cells] = jnp.where(match & ~odd, 1.0, 0.0).astype(BF16)
    put_ref[:, cells : 2 * cells] = jnp.where(match & odd, 1.0, 0.0).astype(BF16)


def rows_kernel(nx, ny, count, c_ref, base_ref, info_ref, pick_ref, put_ref, arr_ref, out_ref):
    cells = c_ref.shape[0]
    side = arr_ref.shape[1] - 8
    wx = wy = side
    devices = out_ref.shape[0]
    lane = lanes_of(count)
    first = spread_matrix(count)

    def unpack(low):
        return low + pltpu.roll(low, LANES - HALF, 1)

    def repeat(edge):
        return jnp.broadcast_to(edge[:, None, :], (wx, wy, LANES)).reshape(cells, LANES)

    near = neighbours(nx, ny)
    there = [jnp.where(ok, 1.0, 0.0) for _, ok in near]
    edge_l = [jnp.where(ok, arr_ref[n, 0:side, :].astype(F32), 0.0) for n, ok in near]
    tiles = [jnp.where(ok, arr_ref[n, side : side + 8, :].astype(F32), 0.0) for n, ok in near]
    shape = (4 * side, 4 * 8)
    cell, tile = iota(shape, 0), iota(shape, 1)
    back = ((tile >> 3) == cell // side) & ((tile & 7) == 4 + ((cell & (side - 1)) >> 2))
    edge_c = dot(back.astype(F32).astype(BF16), jnp.concatenate(tiles, 0).astype(BF16))
    edge_c = jnp.where(own_lanes(4 * side), edge_c, 0.0).astype(BF16)
    edge_c = unpack(dot(edge_c, repeat_lanes(), NT))

    far = dot(pick_ref[...], arr_ref[:, side:, :].reshape(devices * 8, LANES))
    far_l, far_c = far[0:cells], unpack(far[cells:])

    edges = [pl.ds(0, wy), pl.ds(cells - wy, wy), pl.ds(0, wx, stride=wy), pl.ds(wy - 1, wx, stride=wy)]
    self_c = [c_ref[rows, :] for rows in edges]
    start = 5 * cells
    edges = [pl.ds(start, wy), pl.ds(start + cells - wy, wy), pl.ds(start, wx, stride=wy), pl.ds(start + wy - 1, wx, stride=wy)]
    self_l = jnp.concatenate([base_ref[rows, :] for rows in edges], 0)

    def col(value, name):
        return value[:, lane[name] : lane[name] + 1]

    t, w = [], []
    for i, (trans, up) in enumerate([("tx", "ux"), ("tx", "ux"), ("ty", "uy"), ("ty", "uy")]):
        other = edge_c[i * side : (i + 1) * side]
        t.append(col(other, trans) if i % 2 == 0 else col(self_c[i], trans) * there[i])
        w.append(1.0 - col(other, up) if i % 2 == 0 else col(self_c[i], up))
    t, w = jnp.concatenate(t, 0), jnp.concatenate(w, 0)
    share, moved, columns = coupling(jnp.concatenate(self_c, 0), self_l, jnp.concatenate(edge_l, 0), edge_c, t, w)
    part = spread(columns, first)
    off = moved - part
    add = share * self_l + part

    deriv = base_ref[start : start + cells, :]
    far_share, far_moved, far_columns = coupling(c_ref[...], deriv, far_l, far_c, info_ref[:, 1:2], info_ref[:, 2:3])
    far_part = spread(far_columns, first)

    at_y = iota((cells, 1), 0) & (wy - 1)
    low_y, high_y = at_y == 0, at_y == wy - 1

    def edge(value, i):
        return value[i * side : (i + 1) * side]

    def block(i):
        return base_ref[i * cells : (i + 1) * cells, :]

    diag = block(0) + far_share * deriv + far_part
    diag = diag + jnp.where(low_y, repeat(edge(add, 2)), 0.0) + jnp.where(high_y, repeat(edge(add, 3)), 0.0)
    diag = diag + jnp.concatenate([edge(add, 0), jnp.zeros((cells - 2 * wy, LANES), F32), edge(add, 1)], 0)
    xl, xh = block(1), block(2)
    xl = jnp.concatenate([xl[0:wy] + edge(off, 0), xl[wy:]], 0)
    xh = jnp.concatenate([xh[0 : cells - wy], xh[cells - wy :] + edge(off, 1)], 0)
    yl = jnp.where(low_y, repeat(edge(off, 2)), block(3))
    yh = jnp.where(high_y, repeat(edge(off, 3)), block(4))
    blocks = [value.astype(BF16) for value in (diag, xl, xh, yl, yh, far_moved - far_part)]
    pairs = [jnp.concatenate(blocks[i : i + 2], 0) for i in range(0, SENT, 2)]
    placed = dot(put_ref[...], jnp.concatenate(pairs, 1))
    for i in range(SENT // 2):
        part = placed[:, i * LANES : (i + 1) * LANES]
        out_ref[:, i * 8 : (i + 1) * 8, :] = part.reshape(devices, 8, LANES).astype(BF16)


def expand_kernel(count, in_ref, out_ref, full_ref, sems):
    chunks = sems.shape[0]
    wide = out_ref.shape[2]
    group = 8
    tall, deep = group * 4 * BLOCKS, group * 4 * SENT
    o, i = iota((tall, deep), 0), iota((tall, deep), 1)
    block = o & 7
    want = (o >> 5) * (SENT * 4) + jnp.where(block == 7, 5, block) * 4 + ((o >> 3) & 3)
    order = ((block != 5) & (block != 6) & (i == want)).astype(F32).astype(BF16)
    src, to = iota((LANES, wide), 0), iota((LANES, wide), 1)
    r, c = to // PAD, to % PAD
    widen = ((r < count) & (c < count) & (src == r * count + c)).astype(F32).astype(BF16)
    groups = in_ref.shape[0] // deep
    per = tall // BLOCKS
    span = groups // chunks
    copies = []
    for chunk in range(chunks):
        for g in range(chunk * span, (chunk + 1) * span):
            rows = dot(in_ref[g * deep : (g + 1) * deep, :], widen).astype(BF16)
            full_ref[g * per : (g + 1) * per] = dot(order, rows).reshape(per, BLOCKS, wide).astype(BF16)
        part = pl.ds(chunk * span * per, span * per)
        copy = pltpu.make_async_copy(full_ref.at[part], out_ref.at[part], sems.at[chunk])
        copy.start()
        copies.append(copy)
    for copy in copies:
        copy.wait()


def body(pressure, mobility, mob_deriv, accum, trans, upwind, fault_send, fault_cell, fault_slot, fault_trans, fault_up, cell_owner):
    wx, wy, _ = pressure.shape
    count = mobility.shape[0]
    cells = wx * wy
    nx, ny = lax.axis_size("tx"), lax.axis_size("ty")
    devices = nx * ny
    deriv = jnp.transpose(mob_deriv, (1, 2, 3, 0)).reshape(cells, count * count)
    accumulated = jnp.transpose(accum, (1, 2, 3, 0)).reshape(cells, count * count)
    side = max(wx, wy)
    scal, outgoing = pl.pallas_call(
        functools.partial(pack_kernel, nx, ny),
        out_shape=(
            jax.ShapeDtypeStruct((cells, LANES), F32),
            jax.ShapeDtypeStruct((devices, side + 8, LANES), BF16),
        ),
        scratch_shapes=[pltpu.VMEM((cells, LANES), F32), pltpu.VMEM((cells, LANES), F32)],
        name="pack",
    )(pressure[..., 0], mobility[..., 0], trans[..., 0], upwind[..., 0], deriv, fault_send[0].T)
    arrived = lax.all_to_all(outgoing, ("tx", "ty"), split_axis=0, concat_axis=0, tiled=True)
    base, info, pick, put = pl.pallas_call(
        functools.partial(local_kernel, count, devices, wx, wy),
        out_shape=(
            jax.ShapeDtypeStruct((6 * cells, LANES), F32),
            jax.ShapeDtypeStruct((cells, 8), F32),
            jax.ShapeDtypeStruct((2 * cells, devices * 8), BF16),
            jax.ShapeDtypeStruct((devices * 8, 2 * cells), BF16),
        ),
        scratch_shapes=[pltpu.VMEM((cells, LANES), F32)],
        compiler_params=pltpu.CompilerParams(vmem_limit_bytes=12 << 20),
        cost_estimate=pl.CostEstimate(flops=2 << 27, bytes_accessed=8 << 20, transcendentals=0),
        name="local",
    )(
        scal, deriv, accumulated,
        fault_cell, fault_slot, fault_trans, fault_up, cell_owner.reshape(1, cells),
    )
    buffer = pl.pallas_call(
        functools.partial(rows_kernel, nx, ny, count),
        out_shape=jax.ShapeDtypeStruct((devices, SENT * 4, LANES), BF16),
        compiler_params=pltpu.CompilerParams(vmem_limit_bytes=16 << 20),
        name="rows",
    )(scal, base, info, pick, put, arrived)
    landed = lax.all_to_all(buffer, ("tx", "ty"), split_axis=0, concat_axis=0, tiled=True)
    landed = landed.reshape(devices * SENT * 4, LANES)
    relaid = jax.ShapeDtypeStruct((devices * 4, BLOCKS, PAD * PAD), BF16)
    chunks = 8
    return pl.pallas_call(
        functools.partial(expand_kernel, count),
        out_shape=relaid,
        out_specs=pl.BlockSpec(memory_space=pl.ANY),
        scratch_shapes=[pltpu.VMEM(relaid.shape, BF16), pltpu.SemaphoreType.DMA((chunks,))],
        compiler_params=pltpu.CompilerParams(vmem_limit_bytes=16 << 20),
        name="expand",
    )(landed)


def solution(mesh):
    in_specs = (
        P("tx", "ty", None),
        P(None, "tx", "ty", None),
        P(None, "tx", "ty", None),
        P(None, "tx", "ty", None),
        P(None, "tx", "ty", None),
        P(None, "tx", "ty", None),
        P(("tx", "ty"), None, None),
        P(("tx", "ty"), None),
        P(("tx", "ty"), None),
        P(("tx", "ty"), None),
        P(("tx", "ty"), None),
        P(("tx", "ty"), None),
    )
    out_specs = P(("tx", "ty"), None, None)
    return jax.shard_map(body, mesh=mesh, in_specs=in_specs, out_specs=out_specs, check_vma=False)
```

```python
import functools

import jax
import jax.numpy as jnp
from jax import lax
from jax.experimental import pallas as pl
from jax.experimental.pallas import tpu as pltpu
from jax.sharding import PartitionSpec as P

PAD = 16
LANES = 128
BLOCKS = 8
SENT = 6
HALF = 16
SLOT = 32
F32 = jnp.float32
BF16 = jnp.bfloat16
EXACT = lax.Precision.HIGHEST


def iota(shape, dim):
    return lax.broadcasted_iota(jnp.int32, shape, dim)


def dot(a, b, contract=((1,), (0,)), precision=None):
    return lax.dot_general(
        a, b, (contract, ((), ())), precision=precision, preferred_element_type=F32
    )


NT = ((1,), (1,))


def lanes_of(count):
    return dict(p=0, m=1, tx=count + 1, ty=count + 2, ux=count + 3, uy=count + 4, here=count + 5)


def neighbours(nx, ny):
    ix, iy = lax.axis_index("tx"), lax.axis_index("ty")
    me = ix * ny + iy
    there = [ix > 0, ix < nx - 1, iy > 0, iy < ny - 1]
    return [(jnp.where(ok, me + step, me), ok) for ok, step in zip(there, (-ny, ny, -1, 1))]


def exact_dot(a, b, contract=((1,), (0,)), split_rhs=False):
    total = None
    value = b if split_rhs else a
    for _ in range(3):
        piece = value.astype(BF16)
        value = value - piece.astype(F32)
        term = dot(a, piece, contract) if split_rhs else dot(piece, b, contract)
        total = term if total is None else total + term
    return total


def onehot(condition):
    return condition.astype(F32).astype(BF16)


def fetch(sources, targets, sems):
    copies = [pltpu.make_async_copy(src, dst, sems.at[i]) for i, (src, dst) in enumerate(zip(sources, targets))]
    for copy in copies:
        copy.start()
    return copies


def pack_kernel(nx, ny, *refs):
    sources, (c_out, out_ref), targets, rest = refs[0:6], refs[6:8], refs[8:14], refs[14:]
    c_ref, ls_ref, ps_ref, far_ref, side_ref, pick_ref, sems, loads = rest
    loads = fetch(sources, targets, loads)
    send_ref, p_ref, m_ref, t_ref, u_ref, l_ref = targets
    wx, wy = p_ref.shape
    cells = wx * wy
    count = m_ref.shape[0]
    attrs = count + 5
    loads[0].wait()
    devices = send_ref.shape[1]
    rows = devices * 8
    send = jnp.concatenate([send_ref[...], jnp.zeros((6, devices), jnp.int32)], 0).astype(F32)
    pick_d = onehot((iota((rows, devices), 0) >> 3) == iota((rows, devices), 1))
    picks = dot(pick_d, send.astype(BF16), NT)
    row = iota((rows, 1), 0)
    picks = jnp.where((row & 1) == 1, picks[:, 1:2], picks[:, 0:1]).astype(jnp.int32)
    picks = jnp.where((row & 4) == 4, -1, picks)
    pick_ref[...] = onehot(iota((rows, cells), 1) == picks)
    for load in loads[1:5]:
        load.wait()
    up = u_ref[0:2].astype(F32)
    field = jnp.concatenate([p_ref[...][None], m_ref[...], t_ref[0:2], up], 0)
    field = field.reshape(attrs * wx, wy)
    pick_y = onehot((iota((cells, wy), 0) & (wy - 1)) == iota((cells, wy), 1))
    spread = exact_dot(pick_y, field, NT, split_rhs=True)
    own_x = (iota(spread.shape, 1) & (wx - 1)) == (iota(spread.shape, 0) // wy)
    spread = jnp.where(own_x, spread, 0.0)
    fold = onehot((iota((attrs * wx, LANES), 0) // wx) == iota((attrs * wx, LANES), 1))
    scal = exact_dot(spread, fold)
    scal = jnp.where(iota(scal.shape, 1) == lanes_of(count)["here"], 1.0, scal)
    c_ref[...] = scal
    keep = pltpu.make_async_copy(c_ref, c_out, sems.at[5])
    keep.start()
    high = scal.astype(BF16).astype(F32)
    ps_ref[...] = jnp.where(iota(scal.shape, 1) < HALF, high, 0.0) + pltpu.roll(scal - high, HALF, 1)

    loads[5].wait()
    ls_ref[...] = jnp.zeros_like(ls_ref)
    ls_ref[:, 0 : l_ref.shape[1]] = l_ref[...]
    side = side_ref.shape[1]
    edges = [pl.ds(0, wy), pl.ds(cells - wy, wy), pl.ds(0, wx, stride=wy), pl.ds(wy - 1, wx, stride=wy)]
    near = neighbours(nx, ny)
    copies = []
    for i, (device, there) in enumerate(near):
        side_ref[i] = ls_ref[edges[i], :].astype(BF16)
        copy = pltpu.make_async_copy(side_ref.at[i], out_ref.at[device, pl.ds(0, side)], sems.at[i])
        copies.append((there, copy))

        @pl.when(there)
        def _():
            copy.start()

    both = jnp.concatenate([ls_ref[...], ps_ref[...]], 1).astype(BF16)
    far = dot(pick_ref[...], both)
    far = jnp.where((row & 2) == 2, far[:, LANES:], far[:, 0:LANES])
    far_ref[...] = far.reshape(devices, 8, LANES).astype(BF16)
    sides = jnp.concatenate([ps_ref[rows_of, :] for rows_of in edges], 0).astype(BF16)
    tiles = dot(gather_tiles(side), jnp.where(own_lanes(4 * side), dot(sides, repeat_lanes()), 0.0).astype(BF16))
    for i, (device, there) in enumerate(near):

        @pl.when(there)
        def _():
            far_ref[device] = (far_ref[device].astype(F32) + tiles[i * 8 : (i + 1) * 8]).astype(BF16)

    copy = pltpu.make_async_copy(far_ref, out_ref.at[:, pl.ds(side, 8)], sems.at[4])
    copy.start()
    copy.wait()
    keep.wait()
    for there, copy in copies:

        @pl.when(there)
        def _():
            copy.wait()


def repeat_lanes():
    return ((iota((LANES, LANES), 1) & (SLOT - 1)) == iota((LANES, LANES), 0)).astype(F32).astype(BF16)


def own_lanes(rows):
    return (iota((rows, LANES), 1) // SLOT) == (iota((rows, LANES), 0) & 3)


def gather_tiles(side):
    shape = (4 * 8, 4 * side)
    tile, cell = iota(shape, 0), iota(shape, 1)
    keep = ((tile >> 3) == cell // side) & ((tile & 7) == 4 + ((cell & (side - 1)) >> 2))
    return keep.astype(F32).astype(BF16)


def spread_matrix(count):
    src, to = iota((LANES, LANES), 0), iota((LANES, LANES), 1)
    keep = (src >= 1) & (src <= count) & (to == (src - 1) * count)
    return keep.astype(F32).astype(BF16)


def spread(columns, matrix):
    high = columns.astype(BF16)
    low = (columns - high.astype(F32)).astype(BF16)
    return dot(high, matrix) + dot(low, matrix)


def coupling(scal, deriv, other_l, other_c, t, w):
    drop = t * (scal[:, 0:1] - other_c[:, 0:1])
    columns = (t * w) * scal + (t * (1.0 - w)) * other_c
    return w * drop, ((1.0 - w) * drop) * other_l, columns


def local_kernel(count, devices, wx, wy, c_ref, l_ref, a_ref, cell_ref, slot_ref, ft_ref, fu_ref, own_ref, base_ref, info_ref, pick_ref, put_ref, ls_ref):
    cells, width = l_ref.shape
    lane = lanes_of(count)
    scal = c_ref[...]
    ls_ref[...] = jnp.zeros_like(ls_ref)
    ls_ref[:, 0:width] = a_ref[...]
    accum = ls_ref[...]
    ls_ref[:, 0:width] = l_ref[...]
    deriv = ls_ref[...]
    at = iota((cells, 1), 0)
    at_x, at_y = at // wy, at & (wy - 1)
    first = spread_matrix(count)

    def col(value, name):
        return value[:, lane[name] : lane[name] + 1]

    scale = jnp.zeros((cells, 1), F32)
    total = jnp.zeros((cells, LANES), F32)
    steps = [(wy, "tx", "ux", at_x == 0), (cells - wy, "tx", "ux", at_x == wx - 1), (1, "ty", "uy", at_y == 0), (cells - 1, "ty", "uy", at_y == wy - 1)]
    for i, (step, trans, up, rim) in enumerate(steps):
        other_c, other_l = pltpu.roll(scal, step, 0), pltpu.roll(deriv, step, 0)
        if i % 2 == 0:
            t, w = col(other_c, trans), 1.0 - col(other_c, up)
        else:
            t, w = col(scal, trans), col(scal, up)
        t = jnp.where(rim, 0.0, t)
        share, moved, columns = coupling(scal, deriv, other_l, other_c, t, w)
        part = spread(columns, first)
        scale = scale + share
        total = total + part
        base_ref[(i + 1) * cells : (i + 2) * cells, :] = moved - part
    base_ref[0:cells, :] = accum + scale * deriv + total
    base_ref[5 * cells : 6 * cells, :] = deriv

    kcell = (iota((cells, cells), 0) == cell_ref[...]).astype(F32)
    info = jnp.concatenate(
        [slot_ref[...].astype(F32), ft_ref[...], fu_ref[...].astype(F32), jnp.zeros((5, cells), F32)], 0
    )
    info = dot(kcell, info, NT, EXACT)
    info_ref[...] = info
    slot = info[:, 0:1].astype(jnp.int32)
    place = (slot >> 1) * 8 + (slot & 1)
    pick_ref[...] = onehot(iota((cells, devices * 8), 1) == place)

    owner = own_ref[...]
    hits = (iota((devices, cells), 0) == owner).astype(F32)
    before = (iota((cells, cells), 0) < iota((cells, cells), 1)).astype(F32).astype(BF16)
    earlier = dot(hits.astype(BF16), before)
    rank = jnp.sum(earlier * hits, 0, keepdims=True)
    target = owner * 4 + rank.astype(jnp.int32)
    row = iota((devices * 8, cells), 0)
    put_ref[...] = onehot(((row >> 3) * 4 + (row & 3)) == target)


def rows_kernel(nx, ny, count, c_ref, base_ref, info_ref, pick_ref, put_ref, arr_ref, out_ref):
    cells = c_ref.shape[0]
    side = arr_ref.shape[1] - 8
    wx = wy = side
    devices = out_ref.shape[0]
    lane = lanes_of(count)
    first = spread_matrix(count)

    def unpack(low):
        return low + pltpu.roll(low, LANES - HALF, 1)

    def repeat(edge):
        return jnp.broadcast_to(edge[:, None, :], (wx, wy, LANES)).reshape(cells, LANES)

    near = neighbours(nx, ny)
    there = [jnp.where(ok, 1.0, 0.0) for _, ok in near]
    edge_l = [jnp.where(ok, arr_ref[n, 0:side, :].astype(F32), 0.0) for n, ok in near]
    tiles = [jnp.where(ok, arr_ref[n, side : side + 8, :].astype(F32), 0.0) for n, ok in near]
    shape = (4 * side, 4 * 8)
    cell, tile = iota(shape, 0), iota(shape, 1)
    back = ((tile >> 3) == cell // side) & ((tile & 7) == 4 + ((cell & (side - 1)) >> 2))
    edge_c = dot(back.astype(F32).astype(BF16), jnp.concatenate(tiles, 0).astype(BF16))
    edge_c = jnp.where(own_lanes(4 * side), edge_c, 0.0).astype(BF16)
    edge_c = unpack(dot(edge_c, repeat_lanes(), NT))

    tail = arr_ref[:, side:, :].astype(F32).reshape(devices * 8, LANES)
    tail = jnp.concatenate([tail.astype(BF16), pltpu.roll(tail, devices * 8 - 2, 0).astype(BF16)], 1)
    far = dot(pick_ref[...], tail)
    far_l, far_c = far[:, 0:LANES], unpack(far[:, LANES:])

    edges = [pl.ds(0, wy), pl.ds(cells - wy, wy), pl.ds(0, wx, stride=wy), pl.ds(wy - 1, wx, stride=wy)]
    self_c = [c_ref[rows, :] for rows in edges]
    start = 5 * cells
    edges = [pl.ds(start, wy), pl.ds(start + cells - wy, wy), pl.ds(start, wx, stride=wy), pl.ds(start + wy - 1, wx, stride=wy)]
    self_l = jnp.concatenate([base_ref[rows, :] for rows in edges], 0)

    def col(value, name):
        return value[:, lane[name] : lane[name] + 1]

    t, w = [], []
    for i, (trans, up) in enumerate([("tx", "ux"), ("tx", "ux"), ("ty", "uy"), ("ty", "uy")]):
        other = edge_c[i * side : (i + 1) * side]
        t.append(col(other, trans) if i % 2 == 0 else col(self_c[i], trans) * there[i])
        w.append(1.0 - col(other, up) if i % 2 == 0 else col(self_c[i], up))
    t, w = jnp.concatenate(t, 0), jnp.concatenate(w, 0)
    share, moved, columns = coupling(jnp.concatenate(self_c, 0), self_l, jnp.concatenate(edge_l, 0), edge_c, t, w)
    part = spread(columns, first)
    off = moved - part
    add = share * self_l + part

    deriv = base_ref[start : start + cells, :]
    far_share, far_moved, far_columns = coupling(c_ref[...], deriv, far_l, far_c, info_ref[:, 1:2], info_ref[:, 2:3])
    far_part = spread(far_columns, first)

    at_y = iota((cells, 1), 0) & (wy - 1)
    low_y, high_y = at_y == 0, at_y == wy - 1

    def edge(value, i):
        return value[i * side : (i + 1) * side]

    def block(i):
        return base_ref[i * cells : (i + 1) * cells, :]

    diag = block(0) + far_share * deriv + far_part
    diag = diag + jnp.where(low_y, repeat(edge(add, 2)), 0.0) + jnp.where(high_y, repeat(edge(add, 3)), 0.0)
    diag = diag + jnp.concatenate([edge(add, 0), jnp.zeros((cells - 2 * wy, LANES), F32), edge(add, 1)], 0)
    xl, xh = block(1), block(2)
    xl = jnp.concatenate([xl[0:wy] + edge(off, 0), xl[wy:]], 0)
    xh = jnp.concatenate([xh[0 : cells - wy], xh[cells - wy :] + edge(off, 1)], 0)
    yl = jnp.where(low_y, repeat(edge(off, 2)), block(3))
    yh = jnp.where(high_y, repeat(edge(off, 3)), block(4))
    blocks = [value.astype(BF16) for value in (diag, xl, xh, yl, yh, far_moved - far_part)]
    odd = (iota((devices * 8, 1), 0) & 4) == 4
    for i in range(SENT // 2):
        pair = dot(put_ref[...], jnp.concatenate(blocks[2 * i : 2 * i + 2], 1))
        part = jnp.where(odd, pair[:, LANES:], pair[:, 0:LANES])
        out_ref[:, i * 8 : (i + 1) * 8, :] = part.reshape(devices, 8, LANES).astype(BF16)


def expand_kernel(count, in_ref, out_ref, full_ref, sems):
    chunks = sems.shape[0]
    wide = out_ref.shape[2]
    group = 8
    tall, deep = group * 4 * BLOCKS, group * 4 * SENT
    o, i = iota((tall, deep), 0), iota((tall, deep), 1)
    block = o & 7
    want = (o >> 5) * (SENT * 4) + jnp.where(block == 7, 5, block) * 4 + ((o >> 3) & 3)
    order = ((block != 5) & (block != 6) & (i == want)).astype(F32).astype(BF16)
    src, to = iota((LANES, wide), 0), iota((LANES, wide), 1)
    r, c = to // PAD, to % PAD
    widen = ((r < count) & (c < count) & (src == r * count + c)).astype(F32).astype(BF16)
    groups = in_ref.shape[0] // deep
    per = tall // BLOCKS
    span = groups // chunks
    copies = []
    for chunk in range(chunks):
        for g in range(chunk * span, (chunk + 1) * span):
            rows = dot(in_ref[g * deep : (g + 1) * deep, :], widen).astype(BF16)
            full_ref[g * per : (g + 1) * per] = dot(order, rows).reshape(per, BLOCKS, wide).astype(BF16)
        part = pl.ds(chunk * span * per, span * per)
        copy = pltpu.make_async_copy(full_ref.at[part], out_ref.at[part], sems.at[chunk])
        copy.start()
        copies.append(copy)
    for copy in copies:
        copy.wait()


def body(pressure, mobility, mob_deriv, accum, trans, upwind, fault_send, fault_cell, fault_slot, fault_trans, fault_up, cell_owner):
    wx, wy, _ = pressure.shape
    count = mobility.shape[0]
    cells = wx * wy
    nx, ny = lax.axis_size("tx"), lax.axis_size("ty")
    devices = nx * ny
    deriv = jnp.transpose(mob_deriv, (1, 2, 3, 0)).reshape(cells, count * count)
    accumulated = jnp.transpose(accum, (1, 2, 3, 0)).reshape(cells, count * count)
    side = max(wx, wy)
    packed = (fault_send[0].T, pressure[..., 0], mobility[..., 0], trans[..., 0], upwind[..., 0], deriv)
    scal, outgoing = pl.pallas_call(
        functools.partial(pack_kernel, nx, ny),
        out_shape=(
            jax.ShapeDtypeStruct((cells, LANES), F32),
            jax.ShapeDtypeStruct((devices, side + 8, LANES), BF16),
        ),
        in_specs=[pl.BlockSpec(memory_space=pl.ANY)] * len(packed),
        out_specs=[pl.BlockSpec(memory_space=pl.ANY)] * 2,
        scratch_shapes=[
            *[pltpu.VMEM(value.shape, value.dtype) for value in packed],
            pltpu.VMEM((cells, LANES), F32),
            pltpu.VMEM((cells, LANES), F32),
            pltpu.VMEM((cells, LANES), F32),
            pltpu.VMEM((devices, 8, LANES), BF16),
            pltpu.VMEM((4, side, LANES), BF16),
            pltpu.VMEM((devices * 8, cells), BF16),
            pltpu.SemaphoreType.DMA((6,)),
            pltpu.SemaphoreType.DMA((len(packed),)),
        ],
        name="pack",
    )(*packed)
    arrived = lax.all_to_all(outgoing, ("tx", "ty"), split_axis=0, concat_axis=0, tiled=True)
    base, info, pick, put = pl.pallas_call(
        functools.partial(local_kernel, count, devices, wx, wy),
        out_shape=(
            jax.ShapeDtypeStruct((6 * cells, LANES), F32),
            jax.ShapeDtypeStruct((cells, 8), F32),
            jax.ShapeDtypeStruct((cells, devices * 8), BF16),
            jax.ShapeDtypeStruct((devices * 8, cells), BF16),
        ),
        scratch_shapes=[pltpu.VMEM((cells, LANES), F32)],
        compiler_params=pltpu.CompilerParams(vmem_limit_bytes=12 << 20),
        cost_estimate=pl.CostEstimate(flops=2 << 27, bytes_accessed=8 << 20, transcendentals=0),
        name="local",
    )(
        scal, deriv, accumulated,
        fault_cell, fault_slot, fault_trans, fault_up, cell_owner.reshape(1, cells),
    )
    buffer = pl.pallas_call(
        functools.partial(rows_kernel, nx, ny, count),
        out_shape=jax.ShapeDtypeStruct((devices, SENT * 4, LANES), BF16),
        compiler_params=pltpu.CompilerParams(vmem_limit_bytes=16 << 20),
        name="rows",
    )(scal, base, info, pick, put, arrived)
    landed = lax.all_to_all(buffer, ("tx", "ty"), split_axis=0, concat_axis=0, tiled=True)
    landed = landed.reshape(devices * SENT * 4, LANES)
    relaid = jax.ShapeDtypeStruct((devices * 4, BLOCKS, PAD * PAD), BF16)
    chunks = 8
    return pl.pallas_call(
        functools.partial(expand_kernel, count),
        out_shape=relaid,
        out_specs=pl.BlockSpec(memory_space=pl.ANY),
        scratch_shapes=[pltpu.VMEM(relaid.shape, BF16), pltpu.SemaphoreType.DMA((chunks,))],
        compiler_params=pltpu.CompilerParams(vmem_limit_bytes=16 << 20),
        name="expand",
    )(landed)


def solution(mesh):
    in_specs = (
        P("tx", "ty", None),
        P(None, "tx", "ty", None),
        P(None, "tx", "ty", None),
        P(None, "tx", "ty", None),
        P(None, "tx", "ty", None),
        P(None, "tx", "ty", None),
        P(("tx", "ty"), None, None),
        P(("tx", "ty"), None),
        P(("tx", "ty"), None),
        P(("tx", "ty"), None),
        P(("tx", "ty"), None),
        P(("tx", "ty"), None),
    )
    out_specs = P(("tx", "ty"), None, None)
    return jax.shard_map(body, mesh=mesh, in_specs=in_specs, out_specs=out_specs, check_vma=False)
```

```python
import functools

import jax
import jax.numpy as jnp
from jax import lax
from jax.experimental import pallas as pl
from jax.experimental.pallas import tpu as pltpu
from jax.sharding import PartitionSpec as P

PAD = 16
LANES = 128
BLOCKS = 8
SENT = 6
SLOT = 14
GROUP = 4
F32 = jnp.float32
BF16 = jnp.bfloat16
EXACT = lax.Precision.HIGHEST


def iota(shape, dim):
    return lax.broadcasted_iota(jnp.int32, shape, dim)


def dot(a, b, contract=((1,), (0,)), precision=None):
    return lax.dot_general(
        a, b, (contract, ((), ())), precision=precision, preferred_element_type=F32
    )


NT = ((1,), (1,))


def lanes_of(count):
    return dict(p=0, m=1, tx=count + 1, ty=count + 2, ux=count + 3, uy=count + 4, here=count + 5)


def neighbours(nx, ny):
    ix, iy = lax.axis_index("tx"), lax.axis_index("ty")
    me = ix * ny + iy
    there = [ix > 0, ix < nx - 1, iy > 0, iy < ny - 1]
    return [(jnp.where(ok, me + step, me), ok) for ok, step in zip(there, (-ny, ny, -1, 1))]


def exact_dot(a, b, contract=((1,), (0,)), split_rhs=False):
    total = None
    value = b if split_rhs else a
    for _ in range(3):
        piece = value.astype(BF16)
        value = value - piece.astype(F32)
        term = dot(a, piece, contract) if split_rhs else dot(piece, b, contract)
        total = term if total is None else total + term
    return total


def onehot(condition):
    return condition.astype(F32).astype(BF16)


def fetch(sources, targets, sems):
    copies = [pltpu.make_async_copy(src, dst, sems.at[i]) for i, (src, dst) in enumerate(zip(sources, targets))]
    for copy in copies:
        copy.start()
    return copies


def pack_kernel(nx, ny, *refs):
    sources, (c_out, out_ref), targets, rest = refs[0:6], refs[6:8], refs[8:14], refs[14:]
    c_ref, ls_ref, ps_ref, far_ref, side_ref, pick_ref, sems, loads = rest
    loads = fetch(sources, targets, loads)
    send_ref, p_ref, m_ref, t_ref, u_ref, l_ref = targets
    wx, wy = p_ref.shape
    cells = wx * wy
    count = m_ref.shape[0]
    attrs = count + 5
    loads[0].wait()
    devices = send_ref.shape[1]
    rows = devices * GROUP
    send = jnp.concatenate([send_ref[...], jnp.zeros((6, devices), jnp.int32)], 0).astype(F32)
    pick_d = onehot((iota((rows, devices), 0) >> 2) == iota((rows, devices), 1))
    picks = dot(pick_d, send.astype(BF16), NT)
    row = iota((rows, 1), 0)
    picks = jnp.where((row & 1) == 1, picks[:, 1:2], picks[:, 0:1]).astype(jnp.int32)
    pick_ref[...] = onehot(iota((rows, cells), 1) == picks)
    for load in loads[1:5]:
        load.wait()
    up = u_ref[0:2].astype(F32)
    field = jnp.concatenate([p_ref[...][None], m_ref[...], t_ref[0:2], up], 0)
    field = field.reshape(attrs * wx, wy)
    pick_y = onehot((iota((cells, wy), 0) & (wy - 1)) == iota((cells, wy), 1))
    spread = exact_dot(pick_y, field, NT, split_rhs=True)
    own_x = (iota(spread.shape, 1) & (wx - 1)) == (iota(spread.shape, 0) // wy)
    spread = jnp.where(own_x, spread, 0.0)
    fold = onehot((iota((attrs * wx, LANES), 0) // wx) == iota((attrs * wx, LANES), 1))
    scal = exact_dot(spread, fold)
    scal = jnp.where(iota(scal.shape, 1) == lanes_of(count)["here"], 1.0, scal)
    c_ref[...] = scal
    keep = pltpu.make_async_copy(c_ref, c_out, sems.at[5])
    keep.start()
    low = scal - scal.astype(BF16).astype(F32)
    spot = iota(scal.shape, 1)
    width = l_ref.shape[1]
    tail = jnp.where(spot == width, pltpu.roll(low, width, 1), pltpu.roll(low, width + 1 - lanes_of(count)["tx"], 1))
    ls_ref[...] = jnp.where((spot >= width) & (spot <= width + 2), tail, 0.0)
    ps_ref[...] = jnp.where(spot >= 8 * SLOT, pltpu.roll(scal, 8 * SLOT, 1), 0.0)

    loads[5].wait()
    ls_ref[:, 0:width] = l_ref[...]
    groups = side_ref.shape[1]
    edges = [pl.ds(0, wy), pl.ds(cells - wy, wy), pl.ds(0, wx, stride=wy), pl.ds(wy - 1, wx, stride=wy)]
    near = neighbours(nx, ny)
    copies = []
    for i, (device, there) in enumerate(near):
        side_ref[i] = ls_ref[edges[i], :].reshape(groups, GROUP, LANES).astype(BF16)
        copy = pltpu.make_async_copy(side_ref.at[i], out_ref.at[device, pl.ds(0, groups)], sems.at[i])
        copies.append((there, copy))

        @pl.when(there)
        def _():
            copy.start()

    both = jnp.concatenate([ls_ref[...], ps_ref[...]], 1).astype(BF16)
    far = dot(pick_ref[...], both)
    far = jnp.where((row & 2) == 2, far[:, LANES:], far[:, 0:LANES])
    far_ref[...] = far.reshape(devices, GROUP, LANES).astype(BF16)
    half = 2 * wx
    sides = [c_ref[rows_of, :].astype(BF16) for rows_of in edges]
    sides = [dot(jnp.concatenate(sides[i : i + 2], 0), repeat_lanes(count, i)) for i in (0, 2)]
    sides = jnp.where(own_lanes(2 * half), jnp.concatenate(sides, 0), 0.0).astype(BF16)
    tiles = dot(gather_tiles((4 * GROUP, 2 * half), 0), sides)
    for i, (device, there) in enumerate(near):

        @pl.when(there)
        def _():
            far_ref[device] = (far_ref[device].astype(F32) + tiles[i * GROUP : (i + 1) * GROUP]).astype(BF16)

    copy = pltpu.make_async_copy(far_ref, out_ref.at[:, groups], sems.at[4])
    copy.start()
    copy.wait()
    keep.wait()
    for there, copy in copies:

        @pl.when(there)
        def _():
            copy.wait()


def cell_of(lane):
    return (lane * 9363) >> 17


def repeat_lanes(count, axis):
    src, to = iota((LANES, LANES), 0), iota((LANES, LANES), 1)
    at = to - cell_of(to) * SLOT
    want = at + jnp.where(at > count + 1, 1, 0)
    if axis:
        want = at + jnp.where(at > count, 1, 0) + jnp.where(at > count + 1, 1, 0)
    return onehot(src == want)


def own_lanes(rows):
    return cell_of(iota((rows, LANES), 1)) == (iota((rows, LANES), 0) & 7)


def gather_tiles(shape, cells_dim):
    tile, cell = iota(shape, cells_dim), iota(shape, 1 - cells_dim)
    return onehot(((tile >> 2) == (cell >> 4)) & ((tile & 3) == 2 + ((cell >> 3) & 1)))


def spread_matrix(count):
    src, to = iota((LANES, LANES), 0), iota((LANES, LANES), 1)
    keep = (src >= 1) & (src <= count) & (to == (src - 1) * count)
    return keep.astype(F32).astype(BF16)


def spread(columns, matrix):
    high = columns.astype(BF16)
    low = (columns - high.astype(F32)).astype(BF16)
    return dot(high, matrix) + dot(low, matrix)


def coupling(scal, deriv, other_l, other_c, t, w):
    drop = t * (scal[:, 0:1] - other_c[:, 0:1])
    columns = (t * w) * scal + (t * (1.0 - w)) * other_c
    return w * drop, ((1.0 - w) * drop) * other_l, columns


def local_kernel(count, devices, wx, wy, c_ref, l_ref, a_ref, cell_ref, slot_ref, ft_ref, fu_ref, own_ref, base_ref, info_ref, pick_ref, put_ref, ls_ref):
    cells, width = l_ref.shape
    lane = lanes_of(count)
    scal = c_ref[...]
    ls_ref[...] = jnp.zeros_like(ls_ref)
    ls_ref[:, 0:width] = a_ref[...]
    accum = ls_ref[...]
    ls_ref[:, 0:width] = l_ref[...]
    deriv = ls_ref[...]
    at = iota((cells, 1), 0)
    at_x, at_y = at // wy, at & (wy - 1)
    first = spread_matrix(count)

    def col(value, name):
        return value[:, lane[name] : lane[name] + 1]

    scale = jnp.zeros((cells, 1), F32)
    total = jnp.zeros((cells, LANES), F32)
    steps = [(wy, "tx", "ux", at_x == 0), (cells - wy, "tx", "ux", at_x == wx - 1), (1, "ty", "uy", at_y == 0), (cells - 1, "ty", "uy", at_y == wy - 1)]
    for i, (step, trans, up, rim) in enumerate(steps):
        other_c, other_l = pltpu.roll(scal, step, 0), pltpu.roll(deriv, step, 0)
        if i % 2 == 0:
            t, w = col(other_c, trans), 1.0 - col(other_c, up)
        else:
            t, w = col(scal, trans), col(scal, up)
        t = jnp.where(rim, 0.0, t)
        share, moved, columns = coupling(scal, deriv, other_l, other_c, t, w)
        part = spread(columns, first)
        scale = scale + share
        total = total + part
        base_ref[(i + 1) * cells : (i + 2) * cells, :] = moved - part
    base_ref[0:cells, :] = accum + scale * deriv + total
    base_ref[5 * cells : 6 * cells, :] = deriv

    kcell = (iota((cells, cells), 0) == cell_ref[...]).astype(F32)
    info = jnp.concatenate(
        [slot_ref[...].astype(F32), ft_ref[...], fu_ref[...].astype(F32), jnp.zeros((5, cells), F32)], 0
    )
    info = dot(kcell, info, NT, EXACT)
    info_ref[...] = info
    slot = info[:, 0:1].astype(jnp.int32)
    place = (slot >> 1) * GROUP + (slot & 1)
    pick_ref[...] = onehot(iota((cells, devices * GROUP), 1) == place)

    owner = own_ref[...]
    hits = (iota((devices, cells), 0) == owner).astype(F32)
    before = (iota((cells, cells), 0) < iota((cells, cells), 1)).astype(F32).astype(BF16)
    earlier = dot(hits.astype(BF16), before)
    rank = jnp.sum(earlier * hits, 0, keepdims=True)
    target = owner * GROUP + rank.astype(jnp.int32)
    put_ref[...] = onehot(iota((devices * GROUP, cells), 0) == target)


def rows_kernel(nx, ny, count, c_ref, base_ref, info_ref, pick_ref, put_ref, arr_ref, out_ref):
    cells = c_ref.shape[0]
    groups = arr_ref.shape[1] - 1
    side = groups * GROUP
    wx = wy = side
    devices = out_ref.shape[0]
    lane = lanes_of(count)
    width = count * count
    first = spread_matrix(count)

    def repeat(edge):
        return jnp.broadcast_to(edge[:, None, :], (wx, wy, LANES)).reshape(cells, LANES)

    def lows(deriv, name, spare):
        moved = pltpu.roll(deriv, LANES + lane[name] - (width + spare), 1)
        return jnp.where(iota(deriv.shape, 1) == lane[name], moved, 0.0)

    near = neighbours(nx, ny)
    there = [jnp.where(ok, 1.0, 0.0) for _, ok in near]
    edge_l = [jnp.where(ok, arr_ref[n, 0:groups].astype(F32).reshape(side, LANES), 0.0) for n, ok in near]
    tiles = [jnp.where(ok, arr_ref[n, groups].astype(F32), 0.0) for n, ok in near]
    packed = dot(gather_tiles((4 * side, 4 * GROUP), 1), jnp.concatenate(tiles, 0).astype(BF16))
    packed = jnp.where(own_lanes(4 * side), packed, 0.0).astype(BF16)
    edge_c = []
    for i, name in ((0, "tx"), (2, "ty")):
        both = jnp.concatenate(edge_l[i : i + 2], 0)
        scal = dot(packed[i * side : (i + 2) * side], repeat_lanes(count, i), NT)
        edge_c.append(scal + lows(both, "p", 0) + lows(both, name, 1 if i == 0 else 2))
    edge_c = jnp.concatenate(edge_c, 0)

    tail = arr_ref[:, groups].astype(F32).reshape(devices * GROUP, LANES)
    tail = jnp.concatenate([tail.astype(BF16), pltpu.roll(tail, devices * GROUP - 2, 0).astype(BF16)], 1)
    far = dot(pick_ref[...], tail)
    far_l = far[:, 0:LANES]
    far_c = pltpu.roll(far[:, LANES:], LANES - 8 * SLOT, 1) + lows(far_l, "p", 0)

    edges = [pl.ds(0, wy), pl.ds(cells - wy, wy), pl.ds(0, wx, stride=wy), pl.ds(wy - 1, wx, stride=wy)]
    self_c = [c_ref[rows, :] for rows in edges]
    start = 5 * cells
    edges = [pl.ds(start, wy), pl.ds(start + cells - wy, wy), pl.ds(start, wx, stride=wy), pl.ds(start + wy - 1, wx, stride=wy)]
    self_l = jnp.concatenate([base_ref[rows, :] for rows in edges], 0)

    def col(value, name):
        return value[:, lane[name] : lane[name] + 1]

    t, w = [], []
    for i, (trans, up) in enumerate([("tx", "ux"), ("tx", "ux"), ("ty", "uy"), ("ty", "uy")]):
        other = edge_c[i * side : (i + 1) * side]
        t.append(col(other, trans) if i % 2 == 0 else col(self_c[i], trans) * there[i])
        w.append(1.0 - col(other, up) if i % 2 == 0 else col(self_c[i], up))
    t, w = jnp.concatenate(t, 0), jnp.concatenate(w, 0)
    share, moved, columns = coupling(jnp.concatenate(self_c, 0), self_l, jnp.concatenate(edge_l, 0), edge_c, t, w)
    part = spread(columns, first)
    off = moved - part
    add = share * self_l + part

    deriv = base_ref[start : start + cells, :]
    far_share, far_moved, far_columns = coupling(c_ref[...], deriv, far_l, far_c, info_ref[:, 1:2], info_ref[:, 2:3])
    far_part = spread(far_columns, first)

    at_y = iota((cells, 1), 0) & (wy - 1)
    low_y, high_y = at_y == 0, at_y == wy - 1

    def edge(value, i):
        return value[i * side : (i + 1) * side]

    def block(i):
        return base_ref[i * cells : (i + 1) * cells, :]

    diag = block(0) + far_share * deriv + far_part
    diag = diag + jnp.where(low_y, repeat(edge(add, 2)), 0.0) + jnp.where(high_y, repeat(edge(add, 3)), 0.0)
    diag = diag + jnp.concatenate([edge(add, 0), jnp.zeros((cells - 2 * wy, LANES), F32), edge(add, 1)], 0)
    xl, xh = block(1), block(2)
    xl = jnp.concatenate([xl[0:wy] + edge(off, 0), xl[wy:]], 0)
    xh = jnp.concatenate([xh[0 : cells - wy], xh[cells - wy :] + edge(off, 1)], 0)
    yl = jnp.where(low_y, repeat(edge(off, 2)), block(3))
    yh = jnp.where(high_y, repeat(edge(off, 3)), block(4))
    blocks = [value.astype(BF16) for value in (diag, xl, xh, yl, yh, far_moved - far_part)]
    for i in range(0, SENT, 2):
        pair = dot(put_ref[...], jnp.concatenate(blocks[i : i + 2], 1)).reshape(devices, GROUP, 2 * LANES)
        out_ref[:, i] = pair[:, :, 0:LANES].astype(BF16)
        out_ref[:, i + 1] = pair[:, :, LANES:].astype(BF16)


def expand_kernel(count, in_ref, out_ref, full_ref, sems):
    chunks = sems.shape[0]
    wide = out_ref.shape[2]
    group = 8
    tall, deep = group * 4 * BLOCKS, group * 4 * SENT
    o, i = iota((tall, deep), 0), iota((tall, deep), 1)
    block = o & 7
    want = (o >> 5) * (SENT * 4) + jnp.where(block == 7, 5, block) * 4 + ((o >> 3) & 3)
    order = ((block != 5) & (block != 6) & (i == want)).astype(F32).astype(BF16)
    src, to = iota((LANES, wide), 0), iota((LANES, wide), 1)
    r, c = to // PAD, to % PAD
    widen = ((r < count) & (c < count) & (src == r * count + c)).astype(F32).astype(BF16)
    groups = in_ref.shape[0] // deep
    per = tall // BLOCKS
    span = groups // chunks
    copies = []
    for chunk in range(chunks):
        for g in range(chunk * span, (chunk + 1) * span):
            rows = dot(order, in_ref[g * deep : (g + 1) * deep, :]).astype(BF16)
            full_ref[g * per : (g + 1) * per] = dot(rows, widen).reshape(per, BLOCKS, wide).astype(BF16)
        part = pl.ds(chunk * span * per, span * per)
        copy = pltpu.make_async_copy(full_ref.at[part], out_ref.at[part], sems.at[chunk])
        copy.start()
        copies.append(copy)
    for copy in copies:
        copy.wait()


def body(pressure, mobility, mob_deriv, accum, trans, upwind, fault_send, fault_cell, fault_slot, fault_trans, fault_up, cell_owner):
    wx, wy, _ = pressure.shape
    count = mobility.shape[0]
    cells = wx * wy
    nx, ny = lax.axis_size("tx"), lax.axis_size("ty")
    devices = nx * ny
    deriv = jnp.transpose(mob_deriv, (1, 2, 3, 0)).reshape(cells, count * count)
    accumulated = jnp.transpose(accum, (1, 2, 3, 0)).reshape(cells, count * count)
    side = max(wx, wy)
    packed = (fault_send[0].T, pressure[..., 0], mobility[..., 0], trans[..., 0], upwind[..., 0], deriv)
    scal, outgoing = pl.pallas_call(
        functools.partial(pack_kernel, nx, ny),
        out_shape=(
            jax.ShapeDtypeStruct((cells, LANES), F32),
            jax.ShapeDtypeStruct((devices, side // GROUP + 1, GROUP, LANES), BF16),
        ),
        in_specs=[pl.BlockSpec(memory_space=pl.ANY)] * len(packed),
        out_specs=[pl.BlockSpec(memory_space=pl.ANY)] * 2,
        scratch_shapes=[
            *[pltpu.VMEM(value.shape, value.dtype) for value in packed],
            pltpu.VMEM((cells, LANES), F32),
            pltpu.VMEM((cells, LANES), F32),
            pltpu.VMEM((cells, LANES), F32),
            pltpu.VMEM((devices, GROUP, LANES), BF16),
            pltpu.VMEM((4, side // GROUP, GROUP, LANES), BF16),
            pltpu.VMEM((devices * GROUP, cells), BF16),
            pltpu.SemaphoreType.DMA((6,)),
            pltpu.SemaphoreType.DMA((len(packed),)),
        ],
        name="pack",
    )(*packed)
    arrived = lax.all_to_all(outgoing, ("tx", "ty"), split_axis=0, concat_axis=0, tiled=True)
    base, info, pick, put = pl.pallas_call(
        functools.partial(local_kernel, count, devices, wx, wy),
        out_shape=(
            jax.ShapeDtypeStruct((6 * cells, LANES), F32),
            jax.ShapeDtypeStruct((cells, 8), F32),
            jax.ShapeDtypeStruct((cells, devices * GROUP), BF16),
            jax.ShapeDtypeStruct((devices * GROUP, cells), BF16),
        ),
        scratch_shapes=[pltpu.VMEM((cells, LANES), F32)],
        compiler_params=pltpu.CompilerParams(vmem_limit_bytes=12 << 20),
        cost_estimate=pl.CostEstimate(flops=2 << 27, bytes_accessed=8 << 20, transcendentals=0),
        name="local",
    )(
        scal, deriv, accumulated,
        fault_cell, fault_slot, fault_trans, fault_up, cell_owner.reshape(1, cells),
    )
    buffer = pl.pallas_call(
        functools.partial(rows_kernel, nx, ny, count),
        out_shape=jax.ShapeDtypeStruct((devices, SENT, GROUP, LANES), BF16),
        compiler_params=pltpu.CompilerParams(vmem_limit_bytes=16 << 20),
        name="rows",
    )(scal, base, info, pick, put, arrived)
    landed = lax.all_to_all(buffer, ("tx", "ty"), split_axis=0, concat_axis=0, tiled=True)
    landed = landed.reshape(devices * SENT * 4, LANES)
    relaid = jax.ShapeDtypeStruct((devices * 4, BLOCKS, PAD * PAD), BF16)
    chunks = 8
    return pl.pallas_call(
        functools.partial(expand_kernel, count),
        out_shape=relaid,
        out_specs=pl.BlockSpec(memory_space=pl.ANY),
        scratch_shapes=[pltpu.VMEM(relaid.shape, BF16), pltpu.SemaphoreType.DMA((chunks,))],
        compiler_params=pltpu.CompilerParams(vmem_limit_bytes=16 << 20),
        name="expand",
    )(landed)


def solution(mesh):
    in_specs = (
        P("tx", "ty", None),
        P(None, "tx", "ty", None),
        P(None, "tx", "ty", None),
        P(None, "tx", "ty", None),
        P(None, "tx", "ty", None),
        P(None, "tx", "ty", None),
        P(("tx", "ty"), None, None),
        P(("tx", "ty"), None),
        P(("tx", "ty"), None),
        P(("tx", "ty"), None),
        P(("tx", "ty"), None),
        P(("tx", "ty"), None),
    )
    out_specs = P(("tx", "ty"), None, None)
    return jax.shard_map(body, mesh=mesh, in_specs=in_specs, out_specs=out_specs, check_vma=False)
```

```python
import functools

import jax
import jax.numpy as jnp
from jax import lax
from jax.experimental import pallas as pl
from jax.experimental.pallas import tpu as pltpu
from jax.sharding import PartitionSpec as P

PAD = 16
LANES = 128
BLOCKS = 8
SENT = 6
SLOT = 14
GROUP = 4
F32 = jnp.float32
BF16 = jnp.bfloat16
EXACT = lax.Precision.HIGHEST


def iota(shape, dim):
    return lax.broadcasted_iota(jnp.int32, shape, dim)


def dot(a, b, contract=((1,), (0,)), precision=None):
    return lax.dot_general(
        a, b, (contract, ((), ())), precision=precision, preferred_element_type=F32
    )


NT = ((1,), (1,))


def lanes_of(count):
    return dict(p=0, m=1, tx=count + 1, ty=count + 2, ux=count + 3, uy=count + 4, here=count + 5)


def first_order(device, nx, ny):
    return (device & (ny - 1)) * nx + device // ny


def neighbours(nx, ny):
    ix, iy = lax.axis_index("tx"), lax.axis_index("ty")
    me = ix * ny + iy
    there = [ix > 0, ix < nx - 1, iy > 0, iy < ny - 1]
    return [(first_order(jnp.where(ok, me + step, me), nx, ny), ok) for ok, step in zip(there, (-ny, ny, -1, 1))]


def onehot(condition):
    return condition.astype(F32).astype(BF16)


def fetch(sources, targets, sems):
    copies = [pltpu.make_async_copy(src, dst, sems.at[i]) for i, (src, dst) in enumerate(zip(sources, targets))]
    for copy in copies:
        copy.start()
    return copies


def pack_kernel(nx, ny, *refs):
    sources, (c_out, out_ref), targets, rest = refs[0:6], refs[6:8], refs[8:14], refs[14:]
    c_ref, ls_ref, ps_ref, far_ref, side_ref, pick_ref, sems, loads = rest
    loads = fetch(sources, targets, loads)
    send_ref, p_ref, m_ref, t_ref, u_ref, l_ref = targets
    wx, wy = p_ref.shape
    cells = wx * wy
    count = m_ref.shape[0]
    attrs = count + 5
    loads[0].wait()
    devices = send_ref.shape[1]
    rows = devices * GROUP
    send = jnp.concatenate([send_ref[...], jnp.zeros((6, devices), jnp.int32)], 0).astype(F32)
    pick_d = onehot((iota((rows, devices), 0) >> 2) == first_order(iota((rows, devices), 1), nx, ny))
    picks = dot(pick_d, send.astype(BF16), NT)
    row = iota((rows, 1), 0)
    picks = jnp.where((row & 1) == 1, picks[:, 1:2], picks[:, 0:1]).astype(jnp.int32)
    pick_ref[...] = onehot(iota((rows, cells), 1) == picks)
    for load in loads[1:5]:
        load.wait()
    up = u_ref[0:2].astype(F32)
    field = jnp.concatenate([p_ref[...][None], m_ref[...], t_ref[0:2], up], 0)
    field = field.reshape(attrs * wx, wy)
    pick_y = onehot((iota((cells, wy), 0) & (wy - 1)) == iota((cells, wy), 1))
    shape = (cells, attrs * wx)
    own_x = (iota(shape, 1) & (wx - 1)) == (iota(shape, 0) // wy)
    high = field.astype(BF16)
    pieces = [high, (field - high.astype(F32)).astype(BF16)]
    pieces = [jnp.where(own_x, dot(pick_y, piece, NT), 0.0).astype(BF16) for piece in pieces]
    fold = iota((2 * attrs * wx, LANES), 0) // wx
    to = iota((2 * attrs * wx, LANES), 1)
    fold = onehot(jnp.where(fold < attrs, fold, fold - attrs + LANES // 2) == to)
    scal = dot(jnp.concatenate(pieces, 1), fold)
    low = pltpu.roll(scal, LANES // 2, 1)
    at = iota(scal.shape, 1)
    low = jnp.where(at < attrs, low, 0.0)
    scal = jnp.where(at < attrs, scal + low, 0.0)
    c_ref[...] = scal
    keep = pltpu.make_async_copy(c_ref, c_out, sems.at[5])
    keep.start()
    low = scal - scal.astype(BF16).astype(F32)
    spot = iota(scal.shape, 1)
    width = l_ref.shape[1]
    tail = jnp.where(spot == width, pltpu.roll(low, width, 1), pltpu.roll(low, width + 1 - lanes_of(count)["tx"], 1))
    ls_ref[...] = jnp.where((spot >= width) & (spot <= width + 2), tail, 0.0)
    ps_ref[...] = jnp.where(spot >= 8 * SLOT, pltpu.roll(scal, 8 * SLOT, 1), 0.0)

    loads[5].wait()
    ls_ref[:, 0:width] = l_ref[...]
    groups = side_ref.shape[1]
    edges = [pl.ds(0, wy), pl.ds(cells - wy, wy), pl.ds(0, wx, stride=wy), pl.ds(wy - 1, wx, stride=wy)]
    near = neighbours(nx, ny)
    copies = []
    for i, (device, there) in enumerate(near):
        side_ref[i] = ls_ref[edges[i], :].reshape(groups, GROUP, LANES).astype(BF16)
        copy = pltpu.make_async_copy(side_ref.at[i], out_ref.at[device, pl.ds(0, groups)], sems.at[i])
        copies.append((there, copy))

        @pl.when(there)
        def _():
            copy.start()

    both = jnp.concatenate([ls_ref[...], ps_ref[...]], 1).astype(BF16)
    far = dot(pick_ref[...], both)
    far = jnp.where((row & 2) == 2, far[:, LANES:], far[:, 0:LANES])
    far_ref[...] = far.reshape(devices, GROUP, LANES).astype(BF16)
    half = 2 * wx
    sides = [c_ref[rows_of, :].astype(BF16) for rows_of in edges]
    sides = [dot(jnp.concatenate(sides[i : i + 2], 0), repeat_lanes(count, i)) for i in (0, 2)]
    sides = jnp.where(own_lanes(2 * half), jnp.concatenate(sides, 0), 0.0).astype(BF16)
    tiles = dot(gather_tiles((4 * GROUP, 2 * half), 0), sides)
    for i, (device, _) in enumerate(near):
        far_ref[device] = (far_ref[device].astype(F32) + tiles[i * GROUP : (i + 1) * GROUP]).astype(BF16)

    copy = pltpu.make_async_copy(far_ref, out_ref.at[:, groups], sems.at[4])
    copy.start()
    copy.wait()
    keep.wait()
    for there, copy in copies:

        @pl.when(there)
        def _():
            copy.wait()


def cell_of(lane):
    return (lane * 9363) >> 17


def repeat_lanes(count, axis):
    src, to = iota((LANES, LANES), 0), iota((LANES, LANES), 1)
    at = to - cell_of(to) * SLOT
    want = at + jnp.where(at > count + 1, 1, 0)
    if axis:
        want = at + jnp.where(at > count, 1, 0) + jnp.where(at > count + 1, 1, 0)
    return onehot(src == want)


def own_lanes(rows):
    return cell_of(iota((rows, LANES), 1)) == (iota((rows, LANES), 0) & 7)


def gather_tiles(shape, cells_dim):
    tile, cell = iota(shape, cells_dim), iota(shape, 1 - cells_dim)
    return onehot(((tile >> 2) == (cell >> 4)) & ((tile & 3) == 2 + ((cell >> 3) & 1)))


def spread_matrix(count):
    src, to = iota((LANES, LANES), 0), iota((LANES, LANES), 1)
    keep = (src >= 1) & (src <= count) & (to == (src - 1) * count)
    return keep.astype(F32).astype(BF16)


def spread(columns, matrix):
    high = columns.astype(BF16)
    low = (columns - high.astype(F32)).astype(BF16)
    return dot(high, matrix) + dot(low, matrix)


def coupling(scal, deriv, other_l, other_c, t, w):
    drop = t * (scal[:, 0:1] - other_c[:, 0:1])
    columns = (t * w) * scal + (t * (1.0 - w)) * other_c
    return w * drop, ((1.0 - w) * drop) * other_l, columns


def local_kernel(count, nx, ny, wx, wy, c_ref, l_ref, a_ref, cell_ref, slot_ref, ft_ref, fu_ref, own_ref, base_ref, info_ref, pick_ref, put_ref, ls_ref):
    cells, width = l_ref.shape
    devices = nx * ny
    lane = lanes_of(count)
    scal = c_ref[...]
    ls_ref[...] = jnp.zeros_like(ls_ref)
    ls_ref[:, 0:width] = a_ref[...]
    accum = ls_ref[...]
    ls_ref[:, 0:width] = l_ref[...]
    deriv = ls_ref[...]
    at = iota((cells, 1), 0)
    at_x, at_y = at // wy, at & (wy - 1)
    first = spread_matrix(count)

    def col(value, name):
        return value[:, lane[name] : lane[name] + 1]

    scale = jnp.zeros((cells, 1), F32)
    total = jnp.zeros((cells, LANES), F32)
    steps = [(wy, "tx", "ux", at_x == 0), (cells - wy, "tx", "ux", at_x == wx - 1), (1, "ty", "uy", at_y == 0), (cells - 1, "ty", "uy", at_y == wy - 1)]
    for i, (step, trans, up, rim) in enumerate(steps):
        other_c, other_l = pltpu.roll(scal, step, 0), pltpu.roll(deriv, step, 0)
        if i % 2 == 0:
            t, w = col(other_c, trans), 1.0 - col(other_c, up)
        else:
            t, w = col(scal, trans), col(scal, up)
        t = jnp.where(rim, 0.0, t)
        share, moved, columns = coupling(scal, deriv, other_l, other_c, t, w)
        part = spread(columns, first)
        scale = scale + share
        total = total + part
        base_ref[(i + 1) * cells : (i + 2) * cells, :] = moved - part
    base_ref[0:cells, :] = accum + scale * deriv + total
    base_ref[5 * cells : 6 * cells, :] = deriv

    kcell = (iota((cells, cells), 0) == cell_ref[...]).astype(F32)
    info = jnp.concatenate(
        [slot_ref[...].astype(F32), ft_ref[...], fu_ref[...].astype(F32), jnp.zeros((5, cells), F32)], 0
    )
    info = dot(kcell, info, NT, EXACT)
    info_ref[...] = info
    slot = info[:, 0:1].astype(jnp.int32)
    place = first_order(slot >> 1, nx, ny) * GROUP + (slot & 1)
    pick_ref[...] = onehot(iota((cells, devices * GROUP), 1) == place)

    owner = own_ref[...]
    hits = (iota((devices, cells), 0) == owner).astype(F32)
    before = (iota((cells, cells), 0) < iota((cells, cells), 1)).astype(F32).astype(BF16)
    earlier = dot(hits.astype(BF16), before)
    rank = jnp.sum(earlier * hits, 0, keepdims=True)
    target = owner * GROUP + rank.astype(jnp.int32)
    put_ref[...] = onehot(iota((devices * GROUP, cells), 0) == target)


def rows_kernel(nx, ny, count, c_ref, base_ref, info_ref, pick_ref, put_ref, arr_ref, out_ref):
    cells = c_ref.shape[0]
    groups = arr_ref.shape[1] - 1
    side = groups * GROUP
    wx = wy = side
    devices = out_ref.shape[0]
    lane = lanes_of(count)
    width = count * count
    first = spread_matrix(count)

    def repeat(edge):
        return jnp.broadcast_to(edge[:, None, :], (wx, wy, LANES)).reshape(cells, LANES)

    def lows(deriv, name, spare):
        moved = pltpu.roll(deriv, LANES + lane[name] - (width + spare), 1)
        return jnp.where(iota(deriv.shape, 1) == lane[name], moved, 0.0)

    near = neighbours(nx, ny)
    there = [jnp.where(ok, 1.0, 0.0) for _, ok in near]
    edge_l = [jnp.where(ok, arr_ref[n, 0:groups].astype(F32).reshape(side, LANES), 0.0) for n, ok in near]
    tiles = [jnp.where(ok, arr_ref[n, groups].astype(F32), 0.0) for n, ok in near]
    packed = dot(gather_tiles((4 * side, 4 * GROUP), 1), jnp.concatenate(tiles, 0).astype(BF16))
    packed = jnp.where(own_lanes(4 * side), packed, 0.0).astype(BF16)
    edge_c = []
    for i, name in ((0, "tx"), (2, "ty")):
        both = jnp.concatenate(edge_l[i : i + 2], 0)
        scal = dot(packed[i * side : (i + 2) * side], repeat_lanes(count, i), NT)
        edge_c.append(scal + lows(both, "p", 0) + lows(both, name, 1 if i == 0 else 2))
    edge_c = jnp.concatenate(edge_c, 0)

    tail = arr_ref[:, groups].astype(F32).reshape(devices * GROUP, LANES)
    tail = jnp.concatenate([tail.astype(BF16), pltpu.roll(tail, devices * GROUP - 2, 0).astype(BF16)], 1)
    far = dot(pick_ref[...], tail)
    far_l = far[:, 0:LANES]
    far_c = pltpu.roll(far[:, LANES:], LANES - 8 * SLOT, 1) + lows(far_l, "p", 0)

    edges = [pl.ds(0, wy), pl.ds(cells - wy, wy), pl.ds(0, wx, stride=wy), pl.ds(wy - 1, wx, stride=wy)]
    self_c = [c_ref[rows, :] for rows in edges]
    start = 5 * cells
    edges = [pl.ds(start, wy), pl.ds(start + cells - wy, wy), pl.ds(start, wx, stride=wy), pl.ds(start + wy - 1, wx, stride=wy)]
    self_l = jnp.concatenate([base_ref[rows, :] for rows in edges], 0)

    def col(value, name):
        return value[:, lane[name] : lane[name] + 1]

    t, w = [], []
    for i, (trans, up) in enumerate([("tx", "ux"), ("tx", "ux"), ("ty", "uy"), ("ty", "uy")]):
        other = edge_c[i * side : (i + 1) * side]
        t.append(col(other, trans) if i % 2 == 0 else col(self_c[i], trans) * there[i])
        w.append(1.0 - col(other, up) if i % 2 == 0 else col(self_c[i], up))
    t, w = jnp.concatenate(t, 0), jnp.concatenate(w, 0)
    share, moved, columns = coupling(jnp.concatenate(self_c, 0), self_l, jnp.concatenate(edge_l, 0), edge_c, t, w)
    part = spread(columns, first)
    off = moved - part
    add = share * self_l + part

    deriv = base_ref[start : start + cells, :]
    far_share, far_moved, far_columns = coupling(c_ref[...], deriv, far_l, far_c, info_ref[:, 1:2], info_ref[:, 2:3])
    far_part = spread(far_columns, first)

    at_y = iota((cells, 1), 0) & (wy - 1)
    low_y, high_y = at_y == 0, at_y == wy - 1

    def edge(value, i):
        return value[i * side : (i + 1) * side]

    def block(i):
        return base_ref[i * cells : (i + 1) * cells, :]

    diag = block(0) + far_share * deriv + far_part
    diag = diag + jnp.where(low_y, repeat(edge(add, 2)), 0.0) + jnp.where(high_y, repeat(edge(add, 3)), 0.0)
    diag = diag + jnp.concatenate([edge(add, 0), jnp.zeros((cells - 2 * wy, LANES), F32), edge(add, 1)], 0)
    xl, xh = block(1), block(2)
    xl = jnp.concatenate([xl[0:wy] + edge(off, 0), xl[wy:]], 0)
    xh = jnp.concatenate([xh[0 : cells - wy], xh[cells - wy :] + edge(off, 1)], 0)
    yl = jnp.where(low_y, repeat(edge(off, 2)), block(3))
    yh = jnp.where(high_y, repeat(edge(off, 3)), block(4))
    blocks = [value.astype(BF16) for value in (diag, xl, xh, yl, yh, far_moved - far_part)]
    for i in range(0, SENT, 2):
        pair = dot(put_ref[...], jnp.concatenate(blocks[i : i + 2], 1)).reshape(devices, GROUP, 2 * LANES)
        out_ref[:, i] = pair[:, :, 0:LANES].astype(BF16)
        out_ref[:, i + 1] = pair[:, :, LANES:].astype(BF16)


def expand_kernel(count, in_ref, out_ref, full_ref, sems):
    chunks = sems.shape[0]
    wide = out_ref.shape[2]
    group = 8
    tall, deep = group * 4 * BLOCKS, group * 4 * SENT
    o, i = iota((tall, deep), 0), iota((tall, deep), 1)
    block = o & 7
    want = (o >> 5) * (SENT * 4) + jnp.where(block == 7, 5, block) * 4 + ((o >> 3) & 3)
    order = ((block != 5) & (block != 6) & (i == want)).astype(F32).astype(BF16)
    src, to = iota((LANES, wide), 0), iota((LANES, wide), 1)
    r, c = to // PAD, to % PAD
    widen = ((r < count) & (c < count) & (src == r * count + c)).astype(F32).astype(BF16)
    groups = in_ref.shape[0] // deep
    per = tall // BLOCKS
    span = groups // chunks
    copies = []
    for chunk in range(chunks):
        for g in range(chunk * span, (chunk + 1) * span):
            rows = dot(order, in_ref[g * deep : (g + 1) * deep, :]).astype(BF16)
            full_ref[g * per : (g + 1) * per] = dot(rows, widen).reshape(per, BLOCKS, wide).astype(BF16)
        part = pl.ds(chunk * span * per, span * per)
        copy = pltpu.make_async_copy(full_ref.at[part], out_ref.at[part], sems.at[chunk])
        copy.start()
        copies.append(copy)
    for copy in copies:
        copy.wait()


def body(pressure, mobility, mob_deriv, accum, trans, upwind, fault_send, fault_cell, fault_slot, fault_trans, fault_up, cell_owner):
    wx, wy, _ = pressure.shape
    count = mobility.shape[0]
    cells = wx * wy
    nx, ny = lax.axis_size("tx"), lax.axis_size("ty")
    devices = nx * ny
    deriv = jnp.transpose(mob_deriv, (1, 2, 3, 0)).reshape(cells, count * count)
    accumulated = jnp.transpose(accum, (1, 2, 3, 0)).reshape(cells, count * count)
    side = max(wx, wy)
    packed = (fault_send[0].T, pressure[..., 0], mobility[..., 0], trans[..., 0], upwind[..., 0], deriv)
    scal, outgoing = pl.pallas_call(
        functools.partial(pack_kernel, nx, ny),
        out_shape=(
            jax.ShapeDtypeStruct((cells, LANES), F32),
            jax.ShapeDtypeStruct((devices, side // GROUP + 1, GROUP, LANES), BF16),
        ),
        in_specs=[pl.BlockSpec(memory_space=pl.ANY)] * len(packed),
        out_specs=[pl.BlockSpec(memory_space=pl.ANY)] * 2,
        scratch_shapes=[
            *[pltpu.VMEM(value.shape, value.dtype) for value in packed],
            pltpu.VMEM((cells, LANES), F32),
            pltpu.VMEM((cells, LANES), F32),
            pltpu.VMEM((cells, LANES), F32),
            pltpu.VMEM((devices, GROUP, LANES), BF16),
            pltpu.VMEM((4, side // GROUP, GROUP, LANES), BF16),
            pltpu.VMEM((devices * GROUP, cells), BF16),
            pltpu.SemaphoreType.DMA((6,)),
            pltpu.SemaphoreType.DMA((len(packed),)),
        ],
        name="pack",
    )(*packed)
    arrived = lax.all_to_all(outgoing, ("ty", "tx"), split_axis=0, concat_axis=0, tiled=True)
    base, info, pick, put = pl.pallas_call(
        functools.partial(local_kernel, count, nx, ny, wx, wy),
        out_shape=(
            jax.ShapeDtypeStruct((6 * cells, LANES), F32),
            jax.ShapeDtypeStruct((cells, 8), F32),
            jax.ShapeDtypeStruct((cells, devices * GROUP), BF16),
            jax.ShapeDtypeStruct((devices * GROUP, cells), BF16),
        ),
        scratch_shapes=[pltpu.VMEM((cells, LANES), F32)],
        compiler_params=pltpu.CompilerParams(vmem_limit_bytes=12 << 20),
        cost_estimate=pl.CostEstimate(flops=2 << 27, bytes_accessed=8 << 20, transcendentals=0),
        name="local",
    )(
        scal, deriv, accumulated,
        fault_cell, fault_slot, fault_trans, fault_up, cell_owner.reshape(1, cells),
    )
    buffer = pl.pallas_call(
        functools.partial(rows_kernel, nx, ny, count),
        out_shape=jax.ShapeDtypeStruct((devices, SENT, GROUP, LANES), BF16),
        compiler_params=pltpu.CompilerParams(vmem_limit_bytes=16 << 20),
        name="rows",
    )(scal, base, info, pick, put, arrived)
    landed = lax.all_to_all(buffer, ("tx", "ty"), split_axis=0, concat_axis=0, tiled=True)
    landed = landed.reshape(devices * SENT * 4, LANES)
    relaid = jax.ShapeDtypeStruct((devices * 4, BLOCKS, PAD * PAD), BF16)
    chunks = 8
    return pl.pallas_call(
        functools.partial(expand_kernel, count),
        out_shape=relaid,
        out_specs=pl.BlockSpec(memory_space=pl.ANY),
        scratch_shapes=[pltpu.VMEM(relaid.shape, BF16), pltpu.SemaphoreType.DMA((chunks,))],
        compiler_params=pltpu.CompilerParams(vmem_limit_bytes=16 << 20),
        name="expand",
    )(landed)


def solution(mesh):
    in_specs = (
        P("tx", "ty", None),
        P(None, "tx", "ty", None),
        P(None, "tx", "ty", None),
        P(None, "tx", "ty", None),
        P(None, "tx", "ty", None),
        P(None, "tx", "ty", None),
        P(("tx", "ty"), None, None),
        P(("tx", "ty"), None),
        P(("tx", "ty"), None),
        P(("tx", "ty"), None),
        P(("tx", "ty"), None),
        P(("tx", "ty"), None),
    )
    out_specs = P(("tx", "ty"), None, None)
    return jax.shard_map(body, mesh=mesh, in_specs=in_specs, out_specs=out_specs, check_vma=False)
```

```python
import functools

import jax
import jax.numpy as jnp
from jax import lax
from jax.experimental import pallas as pl
from jax.experimental.pallas import tpu as pltpu
from jax.sharding import PartitionSpec as P

PAD = 16
LANES = 128
BLOCKS = 8
SENT = 6
SLOT = 14
GROUP = 4
F32 = jnp.float32
BF16 = jnp.bfloat16
EXACT = lax.Precision.HIGHEST


def iota(shape, dim):
    return lax.broadcasted_iota(jnp.int32, shape, dim)


def dot(a, b, contract=((1,), (0,)), precision=None):
    return lax.dot_general(
        a, b, (contract, ((), ())), precision=precision, preferred_element_type=F32
    )


NT = ((1,), (1,))


def lanes_of(count):
    return dict(p=0, m=1, tx=count + 1, ty=count + 2, ux=count + 3, uy=count + 4, here=count + 5)


def first_order(device, nx, ny):
    return (device & (ny - 1)) * nx + device // ny


def neighbours(nx, ny):
    ix, iy = lax.axis_index("tx"), lax.axis_index("ty")
    me = ix * ny + iy
    there = [ix > 0, ix < nx - 1, iy > 0, iy < ny - 1]
    return [(first_order(jnp.where(ok, me + step, me), nx, ny), ok) for ok, step in zip(there, (-ny, ny, -1, 1))]


def onehot(condition):
    return condition.astype(F32).astype(BF16)


def fetch(sources, targets, sems):
    copies = [pltpu.make_async_copy(src, dst, sems.at[i]) for i, (src, dst) in enumerate(zip(sources, targets))]
    for copy in copies:
        copy.start()
    return copies


def pack_kernel(nx, ny, *refs):
    sources, (c_out, out_ref), targets, rest = refs[0:6], refs[6:8], refs[8:14], refs[14:]
    c_ref, ls_ref, ps_ref, far_ref, side_ref, pick_ref, sems, loads = rest
    loads = fetch(sources, targets, loads)
    send_ref, p_ref, m_ref, t_ref, u_ref, l_ref = targets
    wx, wy = p_ref.shape
    cells = wx * wy
    count = m_ref.shape[0]
    attrs = count + 5
    loads[0].wait()
    devices = send_ref.shape[1]
    rows = devices * GROUP
    send = jnp.concatenate([send_ref[...], jnp.zeros((6, devices), jnp.int32)], 0).astype(F32)
    pick_d = onehot((iota((rows, devices), 0) >> 2) == first_order(iota((rows, devices), 1), nx, ny))
    picks = dot(pick_d, send.astype(BF16), NT)
    row = iota((rows, 1), 0)
    picks = jnp.where((row & 1) == 1, picks[:, 1:2], picks[:, 0:1]).astype(jnp.int32)
    pick_ref[...] = onehot(iota((rows, cells), 1) == picks)
    for load in loads[1:5]:
        load.wait()
    up = u_ref[0:2].astype(F32)
    field = jnp.concatenate([p_ref[...][None], m_ref[...], t_ref[0:2], up], 0)
    field = field.reshape(attrs * wx, wy)
    pick_y = onehot((iota((cells, wy), 0) & (wy - 1)) == iota((cells, wy), 1))
    shape = (cells, attrs * wx)
    own_x = (iota(shape, 1) & (wx - 1)) == (iota(shape, 0) // wy)
    high = field.astype(BF16)
    pieces = [high, (field - high.astype(F32)).astype(BF16)]
    pieces = [jnp.where(own_x, dot(pick_y, piece, NT), 0.0).astype(BF16) for piece in pieces]
    fold = iota((2 * attrs * wx, LANES), 0) // wx
    to = iota((2 * attrs * wx, LANES), 1)
    fold = onehot(jnp.where(fold < attrs, fold, fold - attrs + LANES // 2) == to)
    scal = dot(jnp.concatenate(pieces, 1), fold)
    low = pltpu.roll(scal, LANES // 2, 1)
    at = iota(scal.shape, 1)
    low = jnp.where(at < attrs, low, 0.0)
    scal = jnp.where(at < attrs, scal + low, 0.0)
    c_ref[...] = scal
    keep = pltpu.make_async_copy(c_ref, c_out, sems.at[5])
    keep.start()
    low = scal - scal.astype(BF16).astype(F32)
    spot = iota(scal.shape, 1)
    width = l_ref.shape[1]
    tail = jnp.where(spot == width, pltpu.roll(low, width, 1), pltpu.roll(low, width + 1 - lanes_of(count)["tx"], 1))
    ls_ref[...] = jnp.where((spot >= width) & (spot <= width + 2), tail, 0.0)
    ps_ref[...] = jnp.where(spot >= 8 * SLOT, pltpu.roll(scal, 8 * SLOT, 1), 0.0)

    loads[5].wait()
    ls_ref[:, 0:width] = l_ref[...]
    groups = side_ref.shape[1]
    edges = [pl.ds(0, wy), pl.ds(cells - wy, wy), pl.ds(0, wx, stride=wy), pl.ds(wy - 1, wx, stride=wy)]
    near = neighbours(nx, ny)
    copies = []
    for i, (device, there) in enumerate(near):
        side_ref[i] = ls_ref[edges[i], :].reshape(groups, GROUP, LANES).astype(BF16)
        copy = pltpu.make_async_copy(side_ref.at[i], out_ref.at[device, pl.ds(0, groups)], sems.at[i])
        copies.append((there, copy))

        @pl.when(there)
        def _():
            copy.start()

    both = jnp.concatenate([ls_ref[...], ps_ref[...]], 1).astype(BF16)
    far = dot(pick_ref[...], both)
    far = jnp.where((row & 2) == 2, far[:, LANES:], far[:, 0:LANES])
    far_ref[...] = far.reshape(devices, GROUP, LANES).astype(BF16)
    half = 2 * wx
    sides = [c_ref[rows_of, :].astype(BF16) for rows_of in edges]
    sides = [dot(jnp.concatenate(sides[i : i + 2], 0), repeat_lanes(count, i)) for i in (0, 2)]
    sides = jnp.where(own_lanes(2 * half), jnp.concatenate(sides, 0), 0.0).astype(BF16)
    tiles = dot(gather_tiles((4 * GROUP, 2 * half), 0), sides)
    for i, (device, _) in enumerate(near):
        far_ref[device] = (far_ref[device].astype(F32) + tiles[i * GROUP : (i + 1) * GROUP]).astype(BF16)

    copy = pltpu.make_async_copy(far_ref, out_ref.at[:, groups], sems.at[4])
    copy.start()
    copy.wait()
    keep.wait()
    for there, copy in copies:

        @pl.when(there)
        def _():
            copy.wait()


def cell_of(lane):
    return (lane * 9363) >> 17


def repeat_lanes(count, axis):
    src, to = iota((LANES, LANES), 0), iota((LANES, LANES), 1)
    at = to - cell_of(to) * SLOT
    want = at + jnp.where(at > count + 1, 1, 0)
    if axis:
        want = at + jnp.where(at > count, 1, 0) + jnp.where(at > count + 1, 1, 0)
    return onehot(src == want)


def own_lanes(rows):
    return cell_of(iota((rows, LANES), 1)) == (iota((rows, LANES), 0) & 7)


def gather_tiles(shape, cells_dim):
    tile, cell = iota(shape, cells_dim), iota(shape, 1 - cells_dim)
    return onehot(((tile >> 2) == (cell >> 4)) & ((tile & 3) == 2 + ((cell >> 3) & 1)))


def spread_matrix(count):
    src, to = iota((LANES, LANES), 0), iota((LANES, LANES), 1)
    keep = (src >= 1) & (src <= count) & (to == (src - 1) * count)
    return keep.astype(F32).astype(BF16)


def spread(columns, matrix):
    high = columns.astype(BF16)
    low = (columns - high.astype(F32)).astype(BF16)
    return dot(high, matrix) + dot(low, matrix)


def coupling(scal, deriv, other_l, other_c, t, w):
    drop = t * (scal[:, 0:1] - other_c[:, 0:1])
    columns = (t * w) * scal + (t * (1.0 - w)) * other_c
    return w * drop, ((1.0 - w) * drop) * other_l, columns


def local_kernel(count, nx, ny, wx, wy, c_ref, l_ref, a_ref, cell_ref, slot_ref, ft_ref, fu_ref, own_ref, base_ref, info_ref, pick_ref, put_ref, ls_ref):
    cells, width = l_ref.shape
    devices = nx * ny
    lane = lanes_of(count)
    scal = c_ref[...]
    ls_ref[...] = jnp.zeros_like(ls_ref)
    ls_ref[:, 0:width] = a_ref[...]
    accum = ls_ref[...]
    ls_ref[:, 0:width] = l_ref[...]
    deriv = ls_ref[...]
    at = iota((cells, 1), 0)
    at_x, at_y = at // wy, at & (wy - 1)
    first = spread_matrix(count)

    def col(value, name):
        return value[:, lane[name] : lane[name] + 1]

    scale = jnp.zeros((cells, 1), F32)
    total = jnp.zeros((cells, LANES), F32)
    steps = [(wy, "tx", "ux", at_x == 0), (cells - wy, "tx", "ux", at_x == wx - 1), (1, "ty", "uy", at_y == 0), (cells - 1, "ty", "uy", at_y == wy - 1)]
    for i, (step, trans, up, rim) in enumerate(steps):
        other_c, other_l = pltpu.roll(scal, step, 0), pltpu.roll(deriv, step, 0)
        if i % 2 == 0:
            t, w = col(other_c, trans), 1.0 - col(other_c, up)
        else:
            t, w = col(scal, trans), col(scal, up)
        t = jnp.where(rim, 0.0, t)
        share, moved, columns = coupling(scal, deriv, other_l, other_c, t, w)
        part = spread(columns, first)
        scale = scale + share
        total = total + part
        base_ref[(i + 1) * cells : (i + 2) * cells, :] = moved - part
    base_ref[0:cells, :] = accum + scale * deriv + total
    base_ref[5 * cells : 6 * cells, :] = deriv

    kcell = (iota((cells, cells), 0) == cell_ref[...]).astype(F32)
    info = jnp.concatenate(
        [slot_ref[...].astype(F32), ft_ref[...], fu_ref[...].astype(F32), jnp.zeros((5, cells), F32)], 0
    )
    info = dot(kcell, info, NT, EXACT)
    info_ref[...] = info
    slot = info[:, 0:1].astype(jnp.int32)
    place = first_order(slot >> 1, nx, ny) * GROUP + (slot & 1)
    pick_ref[...] = onehot(iota((cells, devices * GROUP), 1) == place)

    owner = own_ref[...]
    hits = (iota((devices, cells), 0) == owner).astype(F32)
    before = (iota((cells, cells), 0) < iota((cells, cells), 1)).astype(F32).astype(BF16)
    earlier = dot(hits.astype(BF16), before)
    rank = jnp.sum(earlier * hits, 0, keepdims=True)
    target = owner * GROUP + rank.astype(jnp.int32)
    put_ref[...] = onehot(iota((devices * GROUP, cells), 0) == target)


def rows_kernel(nx, ny, count, c_ref, base_ref, info_ref, pick_ref, put_ref, arr_ref, out_ref):
    cells = c_ref.shape[0]
    groups = arr_ref.shape[1] - 1
    side = groups * GROUP
    wx = wy = side
    devices = out_ref.shape[0]
    lane = lanes_of(count)
    width = count * count
    first = spread_matrix(count)

    def repeat(edge):
        return jnp.broadcast_to(edge[:, None, :], (wx, wy, LANES)).reshape(cells, LANES)

    def lows(deriv, name, spare):
        moved = pltpu.roll(deriv, LANES + lane[name] - (width + spare), 1)
        return jnp.where(iota(deriv.shape, 1) == lane[name], moved, 0.0)

    near = neighbours(nx, ny)
    there = [jnp.where(ok, 1.0, 0.0) for _, ok in near]
    edge_l = [jnp.where(ok, arr_ref[n, 0:groups].astype(F32).reshape(side, LANES), 0.0) for n, ok in near]
    tiles = [jnp.where(ok, arr_ref[n, groups].astype(F32), 0.0) for n, ok in near]
    packed = dot(gather_tiles((4 * side, 4 * GROUP), 1), jnp.concatenate(tiles, 0).astype(BF16))
    packed = jnp.where(own_lanes(4 * side), packed, 0.0).astype(BF16)
    edge_c = []
    for i, name in ((0, "tx"), (2, "ty")):
        both = jnp.concatenate(edge_l[i : i + 2], 0)
        scal = dot(packed[i * side : (i + 2) * side], repeat_lanes(count, i), NT)
        edge_c.append(scal + lows(both, "p", 0) + lows(both, name, 1 if i == 0 else 2))
    edge_c = jnp.concatenate(edge_c, 0)

    tail = arr_ref[:, groups].astype(F32).reshape(devices * GROUP, LANES)
    tail = jnp.concatenate([tail.astype(BF16), pltpu.roll(tail, devices * GROUP - 2, 0).astype(BF16)], 1)
    far = dot(pick_ref[...], tail)
    far_l = far[:, 0:LANES]
    far_c = pltpu.roll(far[:, LANES:], LANES - 8 * SLOT, 1) + lows(far_l, "p", 0)

    edges = [pl.ds(0, wy), pl.ds(cells - wy, wy), pl.ds(0, wx, stride=wy), pl.ds(wy - 1, wx, stride=wy)]
    self_c = [c_ref[rows, :] for rows in edges]
    start = 5 * cells
    edges = [pl.ds(start, wy), pl.ds(start + cells - wy, wy), pl.ds(start, wx, stride=wy), pl.ds(start + wy - 1, wx, stride=wy)]
    self_l = jnp.concatenate([base_ref[rows, :] for rows in edges], 0)

    def col(value, name):
        return value[:, lane[name] : lane[name] + 1]

    t, w = [], []
    for i, (trans, up) in enumerate([("tx", "ux"), ("tx", "ux"), ("ty", "uy"), ("ty", "uy")]):
        other = edge_c[i * side : (i + 1) * side]
        t.append(col(other, trans) if i % 2 == 0 else col(self_c[i], trans) * there[i])
        w.append(1.0 - col(other, up) if i % 2 == 0 else col(self_c[i], up))
    t, w = jnp.concatenate(t, 0), jnp.concatenate(w, 0)
    share, moved, columns = coupling(jnp.concatenate(self_c, 0), self_l, jnp.concatenate(edge_l, 0), edge_c, t, w)
    part = spread(columns, first)
    off = moved - part
    add = share * self_l + part

    deriv = base_ref[start : start + cells, :]
    far_share, far_moved, far_columns = coupling(c_ref[...], deriv, far_l, far_c, info_ref[:, 1:2], info_ref[:, 2:3])
    far_part = spread(far_columns, first)

    at_y = iota((cells, 1), 0) & (wy - 1)
    low_y, high_y = at_y == 0, at_y == wy - 1

    def edge(value, i):
        return value[i * side : (i + 1) * side]

    def block(i):
        return base_ref[i * cells : (i + 1) * cells, :]

    diag = block(0) + far_share * deriv + far_part
    diag = diag + jnp.where(low_y, repeat(edge(add, 2)), 0.0) + jnp.where(high_y, repeat(edge(add, 3)), 0.0)
    diag = diag + jnp.concatenate([edge(add, 0), jnp.zeros((cells - 2 * wy, LANES), F32), edge(add, 1)], 0)
    xl, xh = block(1), block(2)
    xl = jnp.concatenate([xl[0:wy] + edge(off, 0), xl[wy:]], 0)
    xh = jnp.concatenate([xh[0 : cells - wy], xh[cells - wy :] + edge(off, 1)], 0)
    yl = jnp.where(low_y, repeat(edge(off, 2)), block(3))
    yh = jnp.where(high_y, repeat(edge(off, 3)), block(4))
    blocks = [value.astype(BF16) for value in (diag, xl, xh, yl, yh, far_moved - far_part)]
    for i in range(0, SENT, 2):
        pair = dot(put_ref[...], jnp.concatenate(blocks[i : i + 2], 1)).reshape(devices, GROUP, 2 * LANES)
        out_ref[:, i] = pair[:, :, 0:LANES].astype(BF16)
        out_ref[:, i + 1] = pair[:, :, LANES:].astype(BF16)


def expand_kernel(count, in_ref, out_ref, full_ref, sems):
    chunks = sems.shape[0]
    wide = out_ref.shape[2]
    group = 8
    tall, deep = group * 4 * BLOCKS, group * 4 * SENT
    o, i = iota((tall, deep), 0), iota((tall, deep), 1)
    block = o & 7
    want = (o >> 5) * (SENT * 4) + jnp.where(block == 7, 5, block) * 4 + ((o >> 3) & 3)
    order = ((block != 5) & (block != 6) & (i == want)).astype(F32).astype(BF16)
    src, to = iota((LANES, wide), 0), iota((LANES, wide), 1)
    r, c = to // PAD, to % PAD
    widen = ((r < count) & (c < count) & (src == r * count + c)).astype(F32).astype(BF16)
    groups = in_ref.shape[0] // deep
    per = tall // BLOCKS
    span = groups // chunks
    ordered = []
    for g in range(0, groups, 2):
        pair = [in_ref[h * deep : (h + 1) * deep, :] for h in (g, g + 1)]
        rows = dot(order, jnp.concatenate(pair, 1)).astype(BF16)
        ordered += [rows[:, 0:LANES], rows[:, LANES:]]
    copies = []
    for chunk in range(chunks):
        for g in range(chunk * span, (chunk + 1) * span):
            full = dot(ordered[g], widen)
            full_ref[g * per : (g + 1) * per] = full.reshape(per, BLOCKS, wide).astype(BF16)
        part = pl.ds(chunk * span * per, span * per)
        copy = pltpu.make_async_copy(full_ref.at[part], out_ref.at[part], sems.at[chunk])
        copy.start()
        copies.append(copy)
    for copy in copies:
        copy.wait()


def body(pressure, mobility, mob_deriv, accum, trans, upwind, fault_send, fault_cell, fault_slot, fault_trans, fault_up, cell_owner):
    wx, wy, _ = pressure.shape
    count = mobility.shape[0]
    cells = wx * wy
    nx, ny = lax.axis_size("tx"), lax.axis_size("ty")
    devices = nx * ny
    deriv = jnp.transpose(mob_deriv, (1, 2, 3, 0)).reshape(cells, count * count)
    accumulated = jnp.transpose(accum, (1, 2, 3, 0)).reshape(cells, count * count)
    side = max(wx, wy)
    packed = (fault_send[0].T, pressure[..., 0], mobility[..., 0], trans[..., 0], upwind[..., 0], deriv)
    scal, outgoing = pl.pallas_call(
        functools.partial(pack_kernel, nx, ny),
        out_shape=(
            jax.ShapeDtypeStruct((cells, LANES), F32),
            jax.ShapeDtypeStruct((devices, side // GROUP + 1, GROUP, LANES), BF16),
        ),
        in_specs=[pl.BlockSpec(memory_space=pl.ANY)] * len(packed),
        out_specs=[pl.BlockSpec(memory_space=pl.ANY)] * 2,
        scratch_shapes=[
            *[pltpu.VMEM(value.shape, value.dtype) for value in packed],
            pltpu.VMEM((cells, LANES), F32),
            pltpu.VMEM((cells, LANES), F32),
            pltpu.VMEM((cells, LANES), F32),
            pltpu.VMEM((devices, GROUP, LANES), BF16),
            pltpu.VMEM((4, side // GROUP, GROUP, LANES), BF16),
            pltpu.VMEM((devices * GROUP, cells), BF16),
            pltpu.SemaphoreType.DMA((6,)),
            pltpu.SemaphoreType.DMA((len(packed),)),
        ],
        name="pack",
    )(*packed)
    arrived = lax.all_to_all(outgoing, ("ty", "tx"), split_axis=0, concat_axis=0, tiled=True)
    base, info, pick, put = pl.pallas_call(
        functools.partial(local_kernel, count, nx, ny, wx, wy),
        out_shape=(
            jax.ShapeDtypeStruct((6 * cells, LANES), F32),
            jax.ShapeDtypeStruct((cells, 8), F32),
            jax.ShapeDtypeStruct((cells, devices * GROUP), BF16),
            jax.ShapeDtypeStruct((devices * GROUP, cells), BF16),
        ),
        scratch_shapes=[pltpu.VMEM((cells, LANES), F32)],
        compiler_params=pltpu.CompilerParams(vmem_limit_bytes=12 << 20),
        cost_estimate=pl.CostEstimate(flops=2 << 27, bytes_accessed=8 << 20, transcendentals=0),
        name="local",
    )(
        scal, deriv, accumulated,
        fault_cell, fault_slot, fault_trans, fault_up, cell_owner.reshape(1, cells),
    )
    buffer = pl.pallas_call(
        functools.partial(rows_kernel, nx, ny, count),
        out_shape=jax.ShapeDtypeStruct((devices, SENT, GROUP, LANES), BF16),
        compiler_params=pltpu.CompilerParams(vmem_limit_bytes=16 << 20),
        name="rows",
    )(scal, base, info, pick, put, arrived)
    landed = lax.all_to_all(buffer, ("tx", "ty"), split_axis=0, concat_axis=0, tiled=True)
    landed = landed.reshape(devices * SENT * 4, LANES)
    relaid = jax.ShapeDtypeStruct((devices * 4, BLOCKS, PAD * PAD), BF16)
    chunks = 8
    return pl.pallas_call(
        functools.partial(expand_kernel, count),
        out_shape=relaid,
        out_specs=pl.BlockSpec(memory_space=pl.ANY),
        scratch_shapes=[pltpu.VMEM(relaid.shape, BF16), pltpu.SemaphoreType.DMA((chunks,))],
        compiler_params=pltpu.CompilerParams(vmem_limit_bytes=16 << 20),
        name="expand",
    )(landed)


def solution(mesh):
    in_specs = (
        P("tx", "ty", None),
        P(None, "tx", "ty", None),
        P(None, "tx", "ty", None),
        P(None, "tx", "ty", None),
        P(None, "tx", "ty", None),
        P(None, "tx", "ty", None),
        P(("tx", "ty"), None, None),
        P(("tx", "ty"), None),
        P(("tx", "ty"), None),
        P(("tx", "ty"), None),
        P(("tx", "ty"), None),
        P(("tx", "ty"), None),
    )
    out_specs = P(("tx", "ty"), None, None)
    return jax.shard_map(body, mesh=mesh, in_specs=in_specs, out_specs=out_specs, check_vma=False)
```

```python
import functools

import jax
import jax.numpy as jnp
from jax import lax
from jax.experimental import pallas as pl
from jax.experimental.pallas import tpu as pltpu
from jax.sharding import PartitionSpec as P

PAD = 16
LANES = 128
BLOCKS = 8
SENT = 6
SLOT = 14
GROUP = 4
F32 = jnp.float32
BF16 = jnp.bfloat16
EXACT = lax.Precision.HIGHEST


def iota(shape, dim):
    return lax.broadcasted_iota(jnp.int32, shape, dim)


def dot(a, b, contract=((1,), (0,)), precision=None):
    return lax.dot_general(
        a, b, (contract, ((), ())), precision=precision, preferred_element_type=F32
    )


NT = ((1,), (1,))


def lanes_of(count):
    return dict(p=0, m=1, tx=count + 1, ty=count + 2, ux=count + 3, uy=count + 4, here=count + 5)


def first_order(device, nx, ny):
    return (device & (ny - 1)) * nx + device // ny


def neighbours(nx, ny):
    ix, iy = lax.axis_index("tx"), lax.axis_index("ty")
    me = ix * ny + iy
    there = [ix > 0, ix < nx - 1, iy > 0, iy < ny - 1]
    return [(first_order(jnp.where(ok, me + step, me), nx, ny), ok) for ok, step in zip(there, (-ny, ny, -1, 1))]


def onehot(condition):
    return condition.astype(F32).astype(BF16)


def fetch(sources, targets, sems):
    copies = [pltpu.make_async_copy(src, dst, sems.at[i]) for i, (src, dst) in enumerate(zip(sources, targets))]
    for copy in copies:
        copy.start()
    return copies


def pack_kernel(nx, ny, *refs):
    sources, (c_out, out_ref), targets, rest = refs[0:6], refs[6:8], refs[8:14], refs[14:]
    c_ref, ls_ref, ps_ref, far_ref, side_ref, pick_ref, sems, loads = rest
    loads = fetch(sources, targets, loads)
    send_ref, p_ref, m_ref, t_ref, u_ref, l_ref = targets
    wx, wy = p_ref.shape
    cells = wx * wy
    count = m_ref.shape[0]
    attrs = count + 5
    loads[0].wait()
    devices = send_ref.shape[1]
    rows = devices * GROUP
    send = jnp.concatenate([send_ref[...], jnp.zeros((6, devices), jnp.int32)], 0).astype(F32)
    pick_d = onehot((iota((rows, devices), 0) >> 2) == first_order(iota((rows, devices), 1), nx, ny))
    picks = dot(pick_d, send.astype(BF16), NT)
    row = iota((rows, 1), 0)
    picks = jnp.where((row & 1) == 1, picks[:, 1:2], picks[:, 0:1]).astype(jnp.int32)
    pick_ref[...] = onehot(iota((rows, cells), 1) == picks)
    for load in loads[1:5]:
        load.wait()
    up = u_ref[0:2].astype(F32)
    field = jnp.concatenate([p_ref[...][None], m_ref[...], t_ref[0:2], up], 0)
    field = field.reshape(attrs * wx, wy)
    pick_y = onehot((iota((cells, wy), 0) & (wy - 1)) == iota((cells, wy), 1))
    shape = (cells, attrs * wx)
    own_x = (iota(shape, 1) & (wx - 1)) == (iota(shape, 0) // wy)
    high = field.astype(BF16)
    pieces = [high, (field - high.astype(F32)).astype(BF16)]
    pieces = [jnp.where(own_x, dot(pick_y, piece, NT), 0.0).astype(BF16) for piece in pieces]
    fold = iota((2 * attrs * wx, LANES), 0) // wx
    to = iota((2 * attrs * wx, LANES), 1)
    fold = onehot(jnp.where(fold < attrs, fold, fold - attrs + LANES // 2) == to)
    scal = dot(jnp.concatenate(pieces, 1), fold)
    low = pltpu.roll(scal, LANES // 2, 1)
    at = iota(scal.shape, 1)
    low = jnp.where(at < attrs, low, 0.0)
    scal = jnp.where(at < attrs, scal + low, 0.0)
    c_ref[...] = scal
    keep = pltpu.make_async_copy(c_ref, c_out, sems.at[5])
    keep.start()
    low = scal - scal.astype(BF16).astype(F32)
    spot = iota(scal.shape, 1)
    width = l_ref.shape[1]
    tail = jnp.where(spot == width, pltpu.roll(low, width, 1), pltpu.roll(low, width + 1 - lanes_of(count)["tx"], 1))
    ls_ref[...] = jnp.where((spot >= width) & (spot <= width + 2), tail, 0.0)
    ps_ref[...] = jnp.where(spot >= 8 * SLOT, pltpu.roll(scal, 8 * SLOT, 1), 0.0)

    loads[5].wait()
    ls_ref[:, 0:width] = l_ref[...]
    groups = side_ref.shape[1]
    edges = [pl.ds(0, wy), pl.ds(cells - wy, wy), pl.ds(0, wx, stride=wy), pl.ds(wy - 1, wx, stride=wy)]
    near = neighbours(nx, ny)
    copies = []
    for i, (device, there) in enumerate(near):
        side_ref[i] = ls_ref[edges[i], :].reshape(groups, GROUP, LANES).astype(BF16)
        copy = pltpu.make_async_copy(side_ref.at[i], out_ref.at[device, pl.ds(0, groups)], sems.at[i])
        copies.append((there, copy))

        @pl.when(there)
        def _():
            copy.start()

    both = jnp.concatenate([ls_ref[...], ps_ref[...]], 1).astype(BF16)
    far = dot(pick_ref[...], both)
    far = jnp.where((row & 2) == 2, far[:, LANES:], far[:, 0:LANES])
    far_ref[...] = far.reshape(devices, GROUP, LANES).astype(BF16)
    half = 2 * wx
    sides = [c_ref[rows_of, :].astype(BF16) for rows_of in edges]
    sides = [dot(jnp.concatenate(sides[i : i + 2], 0), repeat_lanes(count, i)) for i in (0, 2)]
    sides = jnp.where(own_lanes(2 * half), jnp.concatenate(sides, 0), 0.0).astype(BF16)
    tiles = dot(gather_tiles((4 * GROUP, 2 * half), 0), sides)
    for i, (device, _) in enumerate(near):
        far_ref[device] = (far_ref[device].astype(F32) + tiles[i * GROUP : (i + 1) * GROUP]).astype(BF16)

    copy = pltpu.make_async_copy(far_ref, out_ref.at[:, groups], sems.at[4])
    copy.start()
    copy.wait()
    keep.wait()
    for there, copy in copies:

        @pl.when(there)
        def _():
            copy.wait()


def cell_of(lane):
    return (lane * 9363) >> 17


def repeat_lanes(count, axis):
    src, to = iota((LANES, LANES), 0), iota((LANES, LANES), 1)
    at = to - cell_of(to) * SLOT
    want = at + jnp.where(at > count + 1, 1, 0)
    if axis:
        want = at + jnp.where(at > count, 1, 0) + jnp.where(at > count + 1, 1, 0)
    return onehot(src == want)


def own_lanes(rows):
    return cell_of(iota((rows, LANES), 1)) == (iota((rows, LANES), 0) & 7)


def gather_tiles(shape, cells_dim):
    tile, cell = iota(shape, cells_dim), iota(shape, 1 - cells_dim)
    return onehot(((tile >> 2) == (cell >> 4)) & ((tile & 3) == 2 + ((cell >> 3) & 1)))


def spread_matrix(count):
    src, to = iota((LANES, LANES), 0), iota((LANES, LANES), 1)
    keep = (src >= 1) & (src <= count) & (to == (src - 1) * count)
    return keep.astype(F32).astype(BF16)


def spread(columns, matrix):
    high = columns.astype(BF16)
    low = (columns - high.astype(F32)).astype(BF16)
    return dot(high, matrix) + dot(low, matrix)


def coupling(scal, deriv, other_l, other_c, t, w):
    drop = t * (scal[:, 0:1] - other_c[:, 0:1])
    columns = (t * w) * scal + (t * (1.0 - w)) * other_c
    return w * drop, ((1.0 - w) * drop) * other_l, columns


def local_kernel(count, nx, ny, wx, wy, c_ref, l_ref, a_ref, cell_ref, slot_ref, ft_ref, fu_ref, own_ref, base_ref, info_ref, pick_ref, put_ref, ls_ref):
    cells, width = l_ref.shape
    devices = nx * ny
    lane = lanes_of(count)
    scal = c_ref[...]
    ls_ref[...] = jnp.zeros_like(ls_ref)
    ls_ref[:, 0:width] = a_ref[...]
    accum = ls_ref[...]
    ls_ref[:, 0:width] = l_ref[...]
    deriv = ls_ref[...]
    at = iota((cells, 1), 0)
    at_x, at_y = at // wy, at & (wy - 1)
    first = spread_matrix(count)

    def col(value, name):
        return value[:, lane[name] : lane[name] + 1]

    scale = jnp.zeros((cells, 1), F32)
    total = jnp.zeros((cells, LANES), F32)
    steps = [(wy, "tx", "ux", at_x == 0), (cells - wy, "tx", "ux", at_x == wx - 1), (1, "ty", "uy", at_y == 0), (cells - 1, "ty", "uy", at_y == wy - 1)]
    for i, (step, trans, up, rim) in enumerate(steps):
        other_c, other_l = pltpu.roll(scal, step, 0), pltpu.roll(deriv, step, 0)
        if i % 2 == 0:
            t, w = col(other_c, trans), 1.0 - col(other_c, up)
        else:
            t, w = col(scal, trans), col(scal, up)
        t = jnp.where(rim, 0.0, t)
        share, moved, columns = coupling(scal, deriv, other_l, other_c, t, w)
        part = spread(columns, first)
        scale = scale + share
        total = total + part
        base_ref[(i + 1) * cells : (i + 2) * cells, :] = moved - part
    base_ref[0:cells, :] = accum + scale * deriv + total
    base_ref[5 * cells : 6 * cells, :] = deriv

    kcell = (iota((cells, cells), 0) == cell_ref[...]).astype(F32)
    info = jnp.concatenate(
        [slot_ref[...].astype(F32), ft_ref[...], fu_ref[...].astype(F32), jnp.zeros((5, cells), F32)], 0
    )
    info = dot(kcell, info, NT, EXACT)
    info_ref[...] = info
    slot = info[:, 0:1].astype(jnp.int32)
    place = first_order(slot >> 1, nx, ny) * GROUP + (slot & 1)
    pick_ref[...] = onehot(iota((cells, devices * GROUP), 1) == place)

    owner = own_ref[...]
    hits = (iota((devices, cells), 0) == owner).astype(F32)
    before = (iota((cells, cells), 0) < iota((cells, cells), 1)).astype(F32).astype(BF16)
    earlier = dot(hits.astype(BF16), before)
    rank = jnp.sum(earlier * hits, 0, keepdims=True)
    target = owner * GROUP + rank.astype(jnp.int32)
    put_ref[...] = onehot(iota((devices * GROUP, cells), 0) == target)


def rows_kernel(nx, ny, count, c_ref, base_ref, info_ref, pick_ref, put_ref, arr_ref, out_ref):
    cells = c_ref.shape[0]
    groups = arr_ref.shape[1] - 1
    side = groups * GROUP
    wx = wy = side
    devices = out_ref.shape[0]
    lane = lanes_of(count)
    width = count * count
    first = spread_matrix(count)

    def repeat(edge):
        return jnp.broadcast_to(edge[:, None, :], (wx, wy, LANES)).reshape(cells, LANES)

    def lows(deriv, name, spare):
        moved = pltpu.roll(deriv, LANES + lane[name] - (width + spare), 1)
        return jnp.where(iota(deriv.shape, 1) == lane[name], moved, 0.0)

    near = neighbours(nx, ny)
    there = [jnp.where(ok, 1.0, 0.0) for _, ok in near]
    edge_l = [jnp.where(ok, arr_ref[n, 0:groups].astype(F32).reshape(side, LANES), 0.0) for n, ok in near]
    tiles = [jnp.where(ok, arr_ref[n, groups].astype(F32), 0.0) for n, ok in near]
    packed = [jnp.broadcast_to(tile[row : row + 1], (8, LANES)) for tile in tiles for row in (2, 3)]
    packed = jnp.concatenate(packed, 0)
    packed = jnp.where(own_lanes(4 * side), packed, 0.0).astype(BF16)
    edge_c = []
    for i, name in ((0, "tx"), (2, "ty")):
        both = jnp.concatenate(edge_l[i : i + 2], 0)
        scal = dot(packed[i * side : (i + 2) * side], repeat_lanes(count, i), NT)
        edge_c.append(scal + lows(both, "p", 0) + lows(both, name, 1 if i == 0 else 2))
    edge_c = jnp.concatenate(edge_c, 0)

    tail = arr_ref[:, groups].astype(F32).reshape(devices * GROUP, LANES)
    tail = jnp.concatenate([tail.astype(BF16), pltpu.roll(tail, devices * GROUP - 2, 0).astype(BF16)], 1)
    far = dot(pick_ref[...], tail)
    far_l = far[:, 0:LANES]
    far_c = pltpu.roll(far[:, LANES:], LANES - 8 * SLOT, 1) + lows(far_l, "p", 0)

    edges = [pl.ds(0, wy), pl.ds(cells - wy, wy), pl.ds(0, wx, stride=wy), pl.ds(wy - 1, wx, stride=wy)]
    self_c = [c_ref[rows, :] for rows in edges]
    start = 5 * cells
    edges = [pl.ds(start, wy), pl.ds(start + cells - wy, wy), pl.ds(start, wx, stride=wy), pl.ds(start + wy - 1, wx, stride=wy)]
    self_l = jnp.concatenate([base_ref[rows, :] for rows in edges], 0)

    def col(value, name):
        return value[:, lane[name] : lane[name] + 1]

    t, w = [], []
    for i, (trans, up) in enumerate([("tx", "ux"), ("tx", "ux"), ("ty", "uy"), ("ty", "uy")]):
        other = edge_c[i * side : (i + 1) * side]
        t.append(col(other, trans) if i % 2 == 0 else col(self_c[i], trans) * there[i])
        w.append(1.0 - col(other, up) if i % 2 == 0 else col(self_c[i], up))
    t, w = jnp.concatenate(t, 0), jnp.concatenate(w, 0)
    share, moved, columns = coupling(jnp.concatenate(self_c, 0), self_l, jnp.concatenate(edge_l, 0), edge_c, t, w)
    part = spread(columns, first)
    off = moved - part
    add = share * self_l + part

    deriv = base_ref[start : start + cells, :]
    far_share, far_moved, far_columns = coupling(c_ref[...], deriv, far_l, far_c, info_ref[:, 1:2], info_ref[:, 2:3])
    far_part = spread(far_columns, first)

    at_y = iota((cells, 1), 0) & (wy - 1)
    low_y, high_y = at_y == 0, at_y == wy - 1

    def edge(value, i):
        return value[i * side : (i + 1) * side]

    def block(i):
        return base_ref[i * cells : (i + 1) * cells, :]

    diag = block(0) + far_share * deriv + far_part
    diag = diag + jnp.where(low_y, repeat(edge(add, 2)), 0.0) + jnp.where(high_y, repeat(edge(add, 3)), 0.0)
    diag = diag + jnp.concatenate([edge(add, 0), jnp.zeros((cells - 2 * wy, LANES), F32), edge(add, 1)], 0)
    xl, xh = block(1), block(2)
    xl = jnp.concatenate([xl[0:wy] + edge(off, 0), xl[wy:]], 0)
    xh = jnp.concatenate([xh[0 : cells - wy], xh[cells - wy :] + edge(off, 1)], 0)
    yl = jnp.where(low_y, repeat(edge(off, 2)), block(3))
    yh = jnp.where(high_y, repeat(edge(off, 3)), block(4))
    blocks = [value.astype(BF16) for value in (diag, xl, xh, yl, yh, far_moved - far_part)]
    for i in range(0, SENT, 2):
        pair = dot(put_ref[...], jnp.concatenate(blocks[i : i + 2], 1)).reshape(devices, GROUP, 2 * LANES)
        out_ref[:, i] = pair[:, :, 0:LANES].astype(BF16)
        out_ref[:, i + 1] = pair[:, :, LANES:].astype(BF16)


def expand_kernel(count, in_ref, out_ref, full_ref, sems):
    chunks = sems.shape[0]
    wide = out_ref.shape[2]
    group = 8
    tall, deep = group * 4 * BLOCKS, group * 4 * SENT
    o, i = iota((tall, deep), 0), iota((tall, deep), 1)
    block = o & 7
    want = (o >> 5) * (SENT * 4) + jnp.where(block == 7, 5, block) * 4 + ((o >> 3) & 3)
    order = ((block != 5) & (block != 6) & (i == want)).astype(F32).astype(BF16)
    src, to = iota((LANES, wide), 0), iota((LANES, wide), 1)
    r, c = to // PAD, to % PAD
    widen = ((r < count) & (c < count) & (src == r * count + c)).astype(F32).astype(BF16)
    groups = in_ref.shape[0] // deep
    per = tall // BLOCKS
    span = groups // chunks
    ordered = []
    for g in range(0, groups, 2):
        pair = [in_ref[h * deep : (h + 1) * deep, :] for h in (g, g + 1)]
        rows = dot(order, jnp.concatenate(pair, 1)).astype(BF16)
        ordered += [rows[:, 0:LANES], rows[:, LANES:]]
    copies = []
    for chunk in range(chunks):
        for g in range(chunk * span, (chunk + 1) * span):
            full = dot(ordered[g], widen)
            full_ref[g * per : (g + 1) * per] = full.reshape(per, BLOCKS, wide).astype(BF16)
        part = pl.ds(chunk * span * per, span * per)
        copy = pltpu.make_async_copy(full_ref.at[part], out_ref.at[part], sems.at[chunk])
        copy.start()
        copies.append(copy)
    for copy in copies:
        copy.wait()


def body(pressure, mobility, mob_deriv, accum, trans, upwind, fault_send, fault_cell, fault_slot, fault_trans, fault_up, cell_owner):
    wx, wy, _ = pressure.shape
    count = mobility.shape[0]
    cells = wx * wy
    nx, ny = lax.axis_size("tx"), lax.axis_size("ty")
    devices = nx * ny
    deriv = jnp.transpose(mob_deriv, (1, 2, 3, 0)).reshape(cells, count * count)
    accumulated = jnp.transpose(accum, (1, 2, 3, 0)).reshape(cells, count * count)
    side = max(wx, wy)
    packed = (fault_send[0].T, pressure[..., 0], mobility[..., 0], trans[..., 0], upwind[..., 0], deriv)
    scal, outgoing = pl.pallas_call(
        functools.partial(pack_kernel, nx, ny),
        out_shape=(
            jax.ShapeDtypeStruct((cells, LANES), F32),
            jax.ShapeDtypeStruct((devices, side // GROUP + 1, GROUP, LANES), BF16),
        ),
        in_specs=[pl.BlockSpec(memory_space=pl.ANY)] * len(packed),
        out_specs=[pl.BlockSpec(memory_space=pl.ANY)] * 2,
        scratch_shapes=[
            *[pltpu.VMEM(value.shape, value.dtype) for value in packed],
            pltpu.VMEM((cells, LANES), F32),
            pltpu.VMEM((cells, LANES), F32),
            pltpu.VMEM((cells, LANES), F32),
            pltpu.VMEM((devices, GROUP, LANES), BF16),
            pltpu.VMEM((4, side // GROUP, GROUP, LANES), BF16),
            pltpu.VMEM((devices * GROUP, cells), BF16),
            pltpu.SemaphoreType.DMA((6,)),
            pltpu.SemaphoreType.DMA((len(packed),)),
        ],
        name="pack",
    )(*packed)
    arrived = lax.all_to_all(outgoing, ("ty", "tx"), split_axis=0, concat_axis=0, tiled=True)
    base, info, pick, put = pl.pallas_call(
        functools.partial(local_kernel, count, nx, ny, wx, wy),
        out_shape=(
            jax.ShapeDtypeStruct((6 * cells, LANES), F32),
            jax.ShapeDtypeStruct((cells, 8), F32),
            jax.ShapeDtypeStruct((cells, devices * GROUP), BF16),
            jax.ShapeDtypeStruct((devices * GROUP, cells), BF16),
        ),
        scratch_shapes=[pltpu.VMEM((cells, LANES), F32)],
        compiler_params=pltpu.CompilerParams(vmem_limit_bytes=12 << 20),
        cost_estimate=pl.CostEstimate(flops=2 << 27, bytes_accessed=8 << 20, transcendentals=0),
        name="local",
    )(
        scal, deriv, accumulated,
        fault_cell, fault_slot, fault_trans, fault_up, cell_owner.reshape(1, cells),
    )
    buffer = pl.pallas_call(
        functools.partial(rows_kernel, nx, ny, count),
        out_shape=jax.ShapeDtypeStruct((devices, SENT, GROUP, LANES), BF16),
        compiler_params=pltpu.CompilerParams(vmem_limit_bytes=16 << 20),
        name="rows",
    )(scal, base, info, pick, put, arrived)
    landed = lax.all_to_all(buffer, ("tx", "ty"), split_axis=0, concat_axis=0, tiled=True)
    landed = landed.reshape(devices * SENT * 4, LANES)
    relaid = jax.ShapeDtypeStruct((devices * 4, BLOCKS, PAD * PAD), BF16)
    chunks = 8
    return pl.pallas_call(
        functools.partial(expand_kernel, count),
        out_shape=relaid,
        out_specs=pl.BlockSpec(memory_space=pl.ANY),
        scratch_shapes=[pltpu.VMEM(relaid.shape, BF16), pltpu.SemaphoreType.DMA((chunks,))],
        compiler_params=pltpu.CompilerParams(vmem_limit_bytes=16 << 20),
        name="expand",
    )(landed)


def solution(mesh):
    in_specs = (
        P("tx", "ty", None),
        P(None, "tx", "ty", None),
        P(None, "tx", "ty", None),
        P(None, "tx", "ty", None),
        P(None, "tx", "ty", None),
        P(None, "tx", "ty", None),
        P(("tx", "ty"), None, None),
        P(("tx", "ty"), None),
        P(("tx", "ty"), None),
        P(("tx", "ty"), None),
        P(("tx", "ty"), None),
        P(("tx", "ty"), None),
    )
    out_specs = P(("tx", "ty"), None, None)
    return jax.shard_map(body, mesh=mesh, in_specs=in_specs, out_specs=out_specs, check_vma=False)
```

```python
import functools

import jax
import jax.numpy as jnp
from jax import lax
from jax.experimental import pallas as pl
from jax.experimental.pallas import tpu as pltpu
from jax.sharding import PartitionSpec as P

PAD = 16
LANES = 128
BLOCKS = 8
SENT = 6
SLOT = 14
GROUP = 4
F32 = jnp.float32
BF16 = jnp.bfloat16
EXACT = lax.Precision.HIGHEST


def iota(shape, dim):
    return lax.broadcasted_iota(jnp.int32, shape, dim)


def dot(a, b, contract=((1,), (0,)), precision=None):
    return lax.dot_general(
        a, b, (contract, ((), ())), precision=precision, preferred_element_type=F32
    )


NT = ((1,), (1,))


def lanes_of(count):
    return dict(p=0, m=1, tx=count + 1, ty=count + 2, ux=count + 3, uy=count + 4, here=count + 5)


def first_order(device, nx, ny):
    return (device & (ny - 1)) * nx + device // ny


def neighbours(nx, ny):
    ix, iy = lax.axis_index("tx"), lax.axis_index("ty")
    me = ix * ny + iy
    there = [ix > 0, ix < nx - 1, iy > 0, iy < ny - 1]
    return [(first_order(jnp.where(ok, me + step, me), nx, ny), ok) for ok, step in zip(there, (-ny, ny, -1, 1))]


def onehot(condition):
    return condition.astype(F32).astype(BF16)


def fetch(sources, targets, sems):
    copies = [pltpu.make_async_copy(src, dst, sems.at[i]) for i, (src, dst) in enumerate(zip(sources, targets))]
    for copy in copies:
        copy.start()
    return copies


def pack_kernel(nx, ny, *refs):
    sources, (c_out, out_ref), targets, rest = refs[0:6], refs[6:8], refs[8:14], refs[14:]
    c_ref, ls_ref, ps_ref, far_ref, side_ref, pick_ref, sems, loads = rest
    loads = fetch(sources, targets, loads)
    send_ref, p_ref, m_ref, t_ref, u_ref, l_ref = targets
    wx, wy = p_ref.shape
    cells = wx * wy
    count = m_ref.shape[0]
    attrs = count + 5
    loads[0].wait()
    devices = send_ref.shape[1]
    rows = devices * GROUP
    send = jnp.concatenate([send_ref[...], jnp.zeros((6, devices), jnp.int32)], 0).astype(F32)
    pick_d = onehot((iota((rows, devices), 0) >> 2) == first_order(iota((rows, devices), 1), nx, ny))
    picks = dot(pick_d, send.astype(BF16), NT)
    row = iota((rows, 1), 0)
    picks = jnp.where((row & 1) == 1, picks[:, 1:2], picks[:, 0:1]).astype(jnp.int32)
    pick_ref[...] = onehot(iota((rows, cells), 1) == picks)
    for load in loads[1:5]:
        load.wait()
    up = u_ref[0:2].astype(F32)
    field = jnp.concatenate([p_ref[...][None], m_ref[...], t_ref[0:2], up], 0)
    field = field.reshape(attrs * wx, wy)
    pick_y = onehot((iota((cells, wy), 0) & (wy - 1)) == iota((cells, wy), 1))
    shape = (cells, attrs * wx)
    own_x = (iota(shape, 1) & (wx - 1)) == (iota(shape, 0) // wy)
    high = field.astype(BF16)
    pieces = [high, (field - high.astype(F32)).astype(BF16)]
    pieces = [jnp.where(own_x, dot(pick_y, piece, NT), 0.0).astype(BF16) for piece in pieces]
    fold = iota((2 * attrs * wx, LANES), 0) // wx
    to = iota((2 * attrs * wx, LANES), 1)
    fold = onehot(jnp.where(fold < attrs, fold, fold - attrs + LANES // 2) == to)
    scal = dot(jnp.concatenate(pieces, 1), fold)
    low = pltpu.roll(scal, LANES // 2, 1)
    at = iota(scal.shape, 1)
    low = jnp.where(at < attrs, low, 0.0)
    scal = jnp.where(at < attrs, scal + low, 0.0)
    c_ref[...] = scal
    keep = pltpu.make_async_copy(c_ref, c_out, sems.at[5])
    keep.start()
    low = scal - scal.astype(BF16).astype(F32)
    spot = iota(scal.shape, 1)
    width = l_ref.shape[1]
    tail = jnp.where(spot == width, pltpu.roll(low, width, 1), pltpu.roll(low, width + 1 - lanes_of(count)["tx"], 1))
    ls_ref[...] = jnp.where((spot >= width) & (spot <= width + 2), tail, 0.0)
    ps_ref[...] = jnp.where(spot >= 8 * SLOT, pltpu.roll(scal, 8 * SLOT, 1), 0.0)

    loads[5].wait()
    ls_ref[:, 0:width] = l_ref[...]
    groups = side_ref.shape[1]
    edges = [pl.ds(0, wy), pl.ds(cells - wy, wy), pl.ds(0, wx, stride=wy), pl.ds(wy - 1, wx, stride=wy)]
    near = neighbours(nx, ny)
    copies = []
    for i, (device, there) in enumerate(near):
        side_ref[i] = ls_ref[edges[i], :].reshape(groups, GROUP, LANES).astype(BF16)
        copy = pltpu.make_async_copy(side_ref.at[i], out_ref.at[device, pl.ds(0, groups)], sems.at[i])
        copies.append((there, copy))

        @pl.when(there)
        def _():
            copy.start()

    both = jnp.concatenate([ls_ref[...], ps_ref[...]], 1).astype(BF16)
    far = dot(pick_ref[...], both)
    far = jnp.where((row & 2) == 2, far[:, LANES:], far[:, 0:LANES])
    far_ref[...] = far.reshape(devices, GROUP, LANES).astype(BF16)
    half = 2 * wx
    sides = [c_ref[rows_of, :].astype(BF16) for rows_of in edges]
    sides = [dot(jnp.concatenate(sides[i : i + 2], 0), repeat_lanes(count, i)) for i in (0, 2)]
    sides = jnp.where(own_lanes(2 * half), jnp.concatenate(sides, 0), 0.0).astype(BF16)
    tiles = dot(gather_tiles((4 * GROUP, 2 * half), 0), sides)
    for i, (device, _) in enumerate(near):
        far_ref[device] = (far_ref[device].astype(F32) + tiles[i * GROUP : (i + 1) * GROUP]).astype(BF16)

    copy = pltpu.make_async_copy(far_ref, out_ref.at[:, groups], sems.at[4])
    copy.start()
    copy.wait()
    keep.wait()
    for there, copy in copies:

        @pl.when(there)
        def _():
            copy.wait()


def cell_of(lane):
    return (lane * 9363) >> 17


def repeat_lanes(count, axis):
    src, to = iota((LANES, LANES), 0), iota((LANES, LANES), 1)
    at = to - cell_of(to) * SLOT
    want = at + jnp.where(at > count + 1, 1, 0)
    if axis:
        want = at + jnp.where(at > count, 1, 0) + jnp.where(at > count + 1, 1, 0)
    return onehot(src == want)


def own_lanes(rows):
    return cell_of(iota((rows, LANES), 1)) == (iota((rows, LANES), 0) & 7)


def gather_tiles(shape, cells_dim):
    tile, cell = iota(shape, cells_dim), iota(shape, 1 - cells_dim)
    return onehot(((tile >> 2) == (cell >> 4)) & ((tile & 3) == 2 + ((cell >> 3) & 1)))


def spread_matrix(count):
    src, to = iota((LANES, LANES), 0), iota((LANES, LANES), 1)
    keep = (src >= 1) & (src <= count) & (to == (src - 1) * count)
    return keep.astype(F32).astype(BF16)


def spread(columns, matrix):
    high = columns.astype(BF16)
    low = (columns - high.astype(F32)).astype(BF16)
    return dot(high, matrix) + dot(low, matrix)


def coupling(scal, deriv, other_l, other_c, t, w):
    drop = t * (scal[:, 0:1] - other_c[:, 0:1])
    columns = (t * w) * scal + (t * (1.0 - w)) * other_c
    return w * drop, ((1.0 - w) * drop) * other_l, columns


def local_kernel(count, nx, ny, wx, wy, c_ref, l_ref, a_ref, cell_ref, slot_ref, ft_ref, fu_ref, own_ref, base_ref, info_ref, pick_ref, put_ref, ls_ref):
    cells, width = l_ref.shape
    devices = nx * ny
    lane = lanes_of(count)
    scal = c_ref[...]
    ls_ref[...] = jnp.zeros_like(ls_ref)
    ls_ref[:, 0:width] = a_ref[...]
    accum = ls_ref[...]
    ls_ref[:, 0:width] = l_ref[...]
    deriv = ls_ref[...]
    at = iota((cells, 1), 0)
    at_x, at_y = at // wy, at & (wy - 1)
    first = spread_matrix(count)

    def col(value, name):
        return value[:, lane[name] : lane[name] + 1]

    scale = jnp.zeros((cells, 1), F32)
    total = jnp.zeros((cells, LANES), F32)
    steps = [(wy, "tx", "ux", at_x == 0), (cells - wy, "tx", "ux", at_x == wx - 1), (1, "ty", "uy", at_y == 0), (cells - 1, "ty", "uy", at_y == wy - 1)]
    for i, (step, trans, up, rim) in enumerate(steps):
        other_c, other_l = pltpu.roll(scal, step, 0), pltpu.roll(deriv, step, 0)
        if i % 2 == 0:
            t, w = col(other_c, trans), 1.0 - col(other_c, up)
        else:
            t, w = col(scal, trans), col(scal, up)
        t = jnp.where(rim, 0.0, t)
        share, moved, columns = coupling(scal, deriv, other_l, other_c, t, w)
        part = spread(columns, first)
        scale = scale + share
        total = total + part
        base_ref[(i + 1) * cells : (i + 2) * cells, :] = moved - part
    base_ref[0:cells, :] = accum + scale * deriv + total
    base_ref[5 * cells : 6 * cells, :] = deriv

    kcell = (iota((cells, cells), 0) == cell_ref[...]).astype(F32)
    info = jnp.concatenate(
        [slot_ref[...].astype(F32), ft_ref[...], fu_ref[...].astype(F32), jnp.zeros((5, cells), F32)], 0
    )
    info = dot(kcell, info, NT, EXACT)
    info_ref[...] = info
    slot = info[:, 0:1].astype(jnp.int32)
    place = first_order(slot >> 1, nx, ny) * GROUP + (slot & 1)
    pick_ref[...] = onehot(iota((cells, devices * GROUP), 1) == place)

    owner = own_ref[...]
    hits = (iota((devices, cells), 0) == owner).astype(F32)
    before = (iota((cells, cells), 0) < iota((cells, cells), 1)).astype(F32).astype(BF16)
    earlier = dot(hits.astype(BF16), before)
    rank = jnp.sum(earlier * hits, 0, keepdims=True)
    target = owner * GROUP + rank.astype(jnp.int32)
    put_ref[...] = onehot(iota((devices * GROUP, cells), 0) == target)


def rows_kernel(nx, ny, count, c_ref, base_ref, info_ref, pick_ref, put_ref, arr_ref, out_ref):
    cells = c_ref.shape[0]
    groups = arr_ref.shape[1] - 1
    side = groups * GROUP
    wx = wy = side
    devices = out_ref.shape[0]
    lane = lanes_of(count)
    width = count * count
    first = spread_matrix(count)

    def repeat(edge):
        return jnp.broadcast_to(edge[:, None, :], (wx, wy, LANES)).reshape(cells, LANES)

    def lows(deriv, name, spare):
        moved = pltpu.roll(deriv, LANES + lane[name] - (width + spare), 1)
        return jnp.where(iota(deriv.shape, 1) == lane[name], moved, 0.0)

    near = neighbours(nx, ny)
    there = [jnp.where(ok, 1.0, 0.0) for _, ok in near]
    edge_l = [jnp.where(ok, arr_ref[n, 0:groups].astype(F32).reshape(side, LANES), 0.0) for n, ok in near]
    tiles = [jnp.where(ok, arr_ref[n, groups].astype(F32), 0.0) for n, ok in near]
    packed = [jnp.broadcast_to(tile[row : row + 1], (8, LANES)) for tile in tiles for row in (2, 3)]
    packed = jnp.concatenate(packed, 0)
    packed = jnp.where(own_lanes(4 * side), packed, 0.0).astype(BF16)
    edge_c = []
    for i, name in ((0, "tx"), (2, "ty")):
        both = jnp.concatenate(edge_l[i : i + 2], 0)
        scal = dot(packed[i * side : (i + 2) * side], repeat_lanes(count, i), NT)
        edge_c.append(scal + lows(both, "p", 0) + lows(both, name, 1 if i == 0 else 2))
    edge_c = jnp.concatenate(edge_c, 0)

    tail = arr_ref[:, groups].astype(F32).reshape(devices * GROUP, LANES)
    tail = jnp.concatenate([tail.astype(BF16), pltpu.roll(tail, devices * GROUP - 2, 0).astype(BF16)], 1)
    far = dot(pick_ref[...], tail)
    far_l = far[:, 0:LANES]
    far_c = pltpu.roll(far[:, LANES:], LANES - 8 * SLOT, 1) + lows(far_l, "p", 0)

    edges = [pl.ds(0, wy), pl.ds(cells - wy, wy), pl.ds(0, wx, stride=wy), pl.ds(wy - 1, wx, stride=wy)]
    self_c = [c_ref[rows, :] for rows in edges]
    start = 5 * cells
    edges = [pl.ds(start, wy), pl.ds(start + cells - wy, wy), pl.ds(start, wx, stride=wy), pl.ds(start + wy - 1, wx, stride=wy)]
    self_l = jnp.concatenate([base_ref[rows, :] for rows in edges], 0)

    def col(value, name):
        return value[:, lane[name] : lane[name] + 1]

    t, w = [], []
    for i, (trans, up) in enumerate([("tx", "ux"), ("tx", "ux"), ("ty", "uy"), ("ty", "uy")]):
        other = edge_c[i * side : (i + 1) * side]
        t.append(col(other, trans) if i % 2 == 0 else col(self_c[i], trans) * there[i])
        w.append(1.0 - col(other, up) if i % 2 == 0 else col(self_c[i], up))
    t, w = jnp.concatenate(t, 0), jnp.concatenate(w, 0)
    share, moved, columns = coupling(jnp.concatenate(self_c, 0), self_l, jnp.concatenate(edge_l, 0), edge_c, t, w)
    part = spread(columns, first)
    off = moved - part
    add = share * self_l + part

    deriv = base_ref[start : start + cells, :]
    far_share, far_moved, far_columns = coupling(c_ref[...], deriv, far_l, far_c, info_ref[:, 1:2], info_ref[:, 2:3])
    far_part = spread(far_columns, first)

    at_y = iota((cells, 1), 0) & (wy - 1)
    low_y, high_y = at_y == 0, at_y == wy - 1

    def edge(value, i):
        return value[i * side : (i + 1) * side]

    def block(i):
        return base_ref[i * cells : (i + 1) * cells, :]

    diag = block(0) + far_share * deriv + far_part
    diag = diag + jnp.where(low_y, repeat(edge(add, 2)), 0.0) + jnp.where(high_y, repeat(edge(add, 3)), 0.0)
    diag = diag + jnp.concatenate([edge(add, 0), jnp.zeros((cells - 2 * wy, LANES), F32), edge(add, 1)], 0)
    xl, xh = block(1), block(2)
    xl = jnp.concatenate([xl[0:wy] + edge(off, 0), xl[wy:]], 0)
    xh = jnp.concatenate([xh[0 : cells - wy], xh[cells - wy :] + edge(off, 1)], 0)
    yl = jnp.where(low_y, repeat(edge(off, 2)), block(3))
    yh = jnp.where(high_y, repeat(edge(off, 3)), block(4))
    blocks = [value.astype(BF16) for value in (diag, xl, xh, yl, yh, far_moved - far_part)]
    for i in range(0, SENT, 2):
        pair = dot(put_ref[...], jnp.concatenate(blocks[i : i + 2], 1)).reshape(devices, GROUP, 2 * LANES)
        out_ref[:, i] = pair[:, :, 0:LANES].astype(BF16)
        out_ref[:, i + 1] = pair[:, :, LANES:].astype(BF16)


def expand_kernel(count, in_ref, out_ref, full_ref, sems):
    chunks = sems.shape[0]
    wide = out_ref.shape[2]
    group = 8
    tall, deep = group * 4 * BLOCKS, group * 4 * SENT
    o, i = iota((tall, deep), 0), iota((tall, deep), 1)
    block = o & 7
    want = (o >> 5) * (SENT * 4) + jnp.where(block == 7, 5, block) * 4 + ((o >> 3) & 3)
    order = ((block != 5) & (block != 6) & (i == want)).astype(F32).astype(BF16)
    src, to = iota((LANES, wide), 0), iota((LANES, wide), 1)
    r, c = to // PAD, to % PAD
    widen = ((r < count) & (c < count) & (src == r * count + c)).astype(F32).astype(BF16)
    groups = in_ref.shape[0] // deep
    per = tall // BLOCKS
    span = groups // chunks
    ordered = []

    def order_pair(g):
        pair = [in_ref[h * deep : (h + 1) * deep, :] for h in (g, g + 1)]
        rows = dot(order, jnp.concatenate(pair, 1)).astype(BF16)
        ordered.extend([rows[:, 0:LANES], rows[:, LANES:]])

    ahead = 2 * 4
    for g in range(0, ahead, 2):
        order_pair(g)
    copies = []
    for chunk in range(chunks):
        if len(ordered) < groups:
            order_pair(len(ordered))
        for g in range(chunk * span, (chunk + 1) * span):
            full = dot(ordered[g], widen)
            full_ref[g * per : (g + 1) * per] = full.reshape(per, BLOCKS, wide).astype(BF16)
        part = pl.ds(chunk * span * per, span * per)
        copy = pltpu.make_async_copy(full_ref.at[part], out_ref.at[part], sems.at[chunk])
        copy.start()
        copies.append(copy)
    for copy in copies:
        copy.wait()


def body(pressure, mobility, mob_deriv, accum, trans, upwind, fault_send, fault_cell, fault_slot, fault_trans, fault_up, cell_owner):
    wx, wy, _ = pressure.shape
    count = mobility.shape[0]
    cells = wx * wy
    nx, ny = lax.axis_size("tx"), lax.axis_size("ty")
    devices = nx * ny
    deriv = jnp.transpose(mob_deriv, (1, 2, 3, 0)).reshape(cells, count * count)
    accumulated = jnp.transpose(accum, (1, 2, 3, 0)).reshape(cells, count * count)
    side = max(wx, wy)
    packed = (fault_send[0].T, pressure[..., 0], mobility[..., 0], trans[..., 0], upwind[..., 0], deriv)
    scal, outgoing = pl.pallas_call(
        functools.partial(pack_kernel, nx, ny),
        out_shape=(
            jax.ShapeDtypeStruct((cells, LANES), F32),
            jax.ShapeDtypeStruct((devices, side // GROUP + 1, GROUP, LANES), BF16),
        ),
        in_specs=[pl.BlockSpec(memory_space=pl.ANY)] * len(packed),
        out_specs=[pl.BlockSpec(memory_space=pl.ANY)] * 2,
        scratch_shapes=[
            *[pltpu.VMEM(value.shape, value.dtype) for value in packed],
            pltpu.VMEM((cells, LANES), F32),
            pltpu.VMEM((cells, LANES), F32),
            pltpu.VMEM((cells, LANES), F32),
            pltpu.VMEM((devices, GROUP, LANES), BF16),
            pltpu.VMEM((4, side // GROUP, GROUP, LANES), BF16),
            pltpu.VMEM((devices * GROUP, cells), BF16),
            pltpu.SemaphoreType.DMA((6,)),
            pltpu.SemaphoreType.DMA((len(packed),)),
        ],
        name="pack",
    )(*packed)
    arrived = lax.all_to_all(outgoing, ("ty", "tx"), split_axis=0, concat_axis=0, tiled=True)
    base, info, pick, put = pl.pallas_call(
        functools.partial(local_kernel, count, nx, ny, wx, wy),
        out_shape=(
            jax.ShapeDtypeStruct((6 * cells, LANES), F32),
            jax.ShapeDtypeStruct((cells, 8), F32),
            jax.ShapeDtypeStruct((cells, devices * GROUP), BF16),
            jax.ShapeDtypeStruct((devices * GROUP, cells), BF16),
        ),
        scratch_shapes=[pltpu.VMEM((cells, LANES), F32)],
        compiler_params=pltpu.CompilerParams(vmem_limit_bytes=12 << 20),
        cost_estimate=pl.CostEstimate(flops=2 << 27, bytes_accessed=8 << 20, transcendentals=0),
        name="local",
    )(
        scal, deriv, accumulated,
        fault_cell, fault_slot, fault_trans, fault_up, cell_owner.reshape(1, cells),
    )
    buffer = pl.pallas_call(
        functools.partial(rows_kernel, nx, ny, count),
        out_shape=jax.ShapeDtypeStruct((devices, SENT, GROUP, LANES), BF16),
        compiler_params=pltpu.CompilerParams(vmem_limit_bytes=16 << 20),
        name="rows",
    )(scal, base, info, pick, put, arrived)
    landed = lax.all_to_all(buffer, ("tx", "ty"), split_axis=0, concat_axis=0, tiled=True)
    landed = landed.reshape(devices * SENT * 4, LANES)
    relaid = jax.ShapeDtypeStruct((devices * 4, BLOCKS, PAD * PAD), BF16)
    chunks = 8
    return pl.pallas_call(
        functools.partial(expand_kernel, count),
        out_shape=relaid,
        out_specs=pl.BlockSpec(memory_space=pl.ANY),
        scratch_shapes=[pltpu.VMEM(relaid.shape, BF16), pltpu.SemaphoreType.DMA((chunks,))],
        compiler_params=pltpu.CompilerParams(vmem_limit_bytes=16 << 20),
        name="expand",
    )(landed)


def solution(mesh):
    in_specs = (
        P("tx", "ty", None),
        P(None, "tx", "ty", None),
        P(None, "tx", "ty", None),
        P(None, "tx", "ty", None),
        P(None, "tx", "ty", None),
        P(None, "tx", "ty", None),
        P(("tx", "ty"), None, None),
        P(("tx", "ty"), None),
        P(("tx", "ty"), None),
        P(("tx", "ty"), None),
        P(("tx", "ty"), None),
        P(("tx", "ty"), None),
    )
    out_specs = P(("tx", "ty"), None, None)
    return jax.shard_map(body, mesh=mesh, in_specs=in_specs, out_specs=out_specs, check_vma=False)
```

```python
import functools

import jax
import jax.numpy as jnp
from jax import lax
from jax.experimental import pallas as pl
from jax.experimental.pallas import tpu as pltpu
from jax.sharding import PartitionSpec as P

PAD = 16
LANES = 128
BLOCKS = 8
SENT = 6
SLOT = 14
GROUP = 4
F32 = jnp.float32
BF16 = jnp.bfloat16
EXACT = lax.Precision.HIGHEST


def iota(shape, dim):
    return lax.broadcasted_iota(jnp.int32, shape, dim)


def dot(a, b, contract=((1,), (0,)), precision=None):
    return lax.dot_general(
        a, b, (contract, ((), ())), precision=precision, preferred_element_type=F32
    )


NT = ((1,), (1,))


def lanes_of(count):
    return dict(p=0, m=1, tx=count + 1, ty=count + 2, ux=count + 3, uy=count + 4, here=count + 5)


def first_order(device, nx, ny):
    return (device & (ny - 1)) * nx + device // ny


def neighbours(nx, ny):
    ix, iy = lax.axis_index("tx"), lax.axis_index("ty")
    me = ix * ny + iy
    there = [ix > 0, ix < nx - 1, iy > 0, iy < ny - 1]
    return [(first_order(jnp.where(ok, me + step, me), nx, ny), ok) for ok, step in zip(there, (-ny, ny, -1, 1))]


def onehot(condition):
    return condition.astype(F32).astype(BF16)


def fetch(sources, targets, sems):
    copies = [pltpu.make_async_copy(src, dst, sems.at[i]) for i, (src, dst) in enumerate(zip(sources, targets))]
    for copy in copies:
        copy.start()
    return copies


def pack_kernel(nx, ny, *refs):
    sources, (c_out, out_ref), targets, rest = refs[0:6], refs[6:8], refs[8:14], refs[14:]
    c_ref, ls_ref, ps_ref, far_ref, side_ref, pick_ref, sems, loads = rest
    loads = fetch(sources, targets, loads)
    send_ref, p_ref, m_ref, t_ref, u_ref, l_ref = targets
    wx, wy = p_ref.shape
    cells = wx * wy
    count = m_ref.shape[0]
    attrs = count + 5
    loads[0].wait()
    devices = send_ref.shape[1]
    rows = devices * GROUP
    send = jnp.concatenate([send_ref[...], jnp.zeros((6, devices), jnp.int32)], 0).astype(F32)
    pick_d = onehot((iota((rows, devices), 0) >> 2) == first_order(iota((rows, devices), 1), nx, ny))
    picks = dot(pick_d, send.astype(BF16), NT)
    row = iota((rows, 1), 0)
    picks = jnp.where((row & 1) == 1, picks[:, 1:2], picks[:, 0:1]).astype(jnp.int32)
    pick_ref[...] = onehot(iota((rows, cells), 1) == picks)
    for load in loads[1:5]:
        load.wait()
    up = u_ref[0:2].astype(F32)
    field = jnp.concatenate([p_ref[...][None], m_ref[...], t_ref[0:2], up], 0)
    field = field.reshape(attrs * wx, wy)
    pick_y = onehot((iota((cells, wy), 0) & (wy - 1)) == iota((cells, wy), 1))
    shape = (cells, attrs * wx)
    own_x = (iota(shape, 1) & (wx - 1)) == (iota(shape, 0) // wy)
    high = field.astype(BF16)
    pieces = [high, (field - high.astype(F32)).astype(BF16)]
    pieces = [jnp.where(own_x, dot(pick_y, piece, NT), 0.0).astype(BF16) for piece in pieces]
    fold = iota((2 * attrs * wx, LANES), 0) // wx
    to = iota((2 * attrs * wx, LANES), 1)
    fold = onehot(jnp.where(fold < attrs, fold, fold - attrs + LANES // 2) == to)
    scal = dot(jnp.concatenate(pieces, 1), fold)
    low = pltpu.roll(scal, LANES // 2, 1)
    at = iota(scal.shape, 1)
    low = jnp.where(at < attrs, low, 0.0)
    scal = jnp.where(at < attrs, scal + low, 0.0)
    c_ref[...] = scal
    keep = pltpu.make_async_copy(c_ref, c_out, sems.at[5])
    keep.start()
    low = scal - scal.astype(BF16).astype(F32)
    spot = iota(scal.shape, 1)
    width = l_ref.shape[1]
    tail = jnp.where(spot == width, pltpu.roll(low, width, 1), pltpu.roll(low, width + 1 - lanes_of(count)["tx"], 1))
    ls_ref[...] = jnp.where((spot >= width) & (spot <= width + 2), tail, 0.0)
    ps_ref[...] = jnp.where(spot >= 8 * SLOT, pltpu.roll(scal, 8 * SLOT, 1), 0.0)

    loads[5].wait()
    ls_ref[:, 0:width] = l_ref[...]
    groups = side_ref.shape[1]
    edges = [pl.ds(0, wy), pl.ds(cells - wy, wy), pl.ds(0, wx, stride=wy), pl.ds(wy - 1, wx, stride=wy)]
    near = neighbours(nx, ny)
    copies = []
    for i, (device, there) in enumerate(near):
        side_ref[i] = ls_ref[edges[i], :].reshape(groups, GROUP, LANES).astype(BF16)
        copy = pltpu.make_async_copy(side_ref.at[i], out_ref.at[device, pl.ds(0, groups)], sems.at[i])
        copies.append((there, copy))

        @pl.when(there)
        def _():
            copy.start()

    both = jnp.concatenate([ls_ref[...], ps_ref[...]], 1).astype(BF16)
    far = dot(pick_ref[...], both)
    far = jnp.where((row & 2) == 2, far[:, LANES:], far[:, 0:LANES])
    far_ref[...] = far.reshape(devices, GROUP, LANES).astype(BF16)
    half = 2 * wx
    sides = [c_ref[rows_of, :].astype(BF16) for rows_of in edges]
    sides = [dot(jnp.concatenate(sides[i : i + 2], 0), repeat_lanes(count, i)) for i in (0, 2)]
    sides = jnp.where(own_lanes(2 * half), jnp.concatenate(sides, 0), 0.0).astype(BF16)
    tiles = dot(gather_tiles((4 * GROUP, 2 * half), 0), sides)
    for i, (device, _) in enumerate(near):
        far_ref[device] = (far_ref[device].astype(F32) + tiles[i * GROUP : (i + 1) * GROUP]).astype(BF16)

    copy = pltpu.make_async_copy(far_ref, out_ref.at[:, groups], sems.at[4])
    copy.start()
    copy.wait()
    keep.wait()
    for there, copy in copies:

        @pl.when(there)
        def _():
            copy.wait()


def cell_of(lane):
    return (lane * 9363) >> 17


def repeat_lanes(count, axis):
    src, to = iota((LANES, LANES), 0), iota((LANES, LANES), 1)
    at = to - cell_of(to) * SLOT
    want = at + jnp.where(at > count + 1, 1, 0)
    if axis:
        want = at + jnp.where(at > count, 1, 0) + jnp.where(at > count + 1, 1, 0)
    return onehot(src == want)


def own_lanes(rows):
    return cell_of(iota((rows, LANES), 1)) == (iota((rows, LANES), 0) & 7)


def gather_tiles(shape, cells_dim):
    tile, cell = iota(shape, cells_dim), iota(shape, 1 - cells_dim)
    return onehot(((tile >> 2) == (cell >> 4)) & ((tile & 3) == 2 + ((cell >> 3) & 1)))


def spread_matrix(count):
    src, to = iota((LANES, LANES), 0), iota((LANES, LANES), 1)
    src = src & (LANES // 2 - 1)
    keep = (src >= 1) & (src <= count) & (to == (src - 1) * count)
    return keep.astype(F32).astype(BF16)


def spread(columns, matrix):
    high = columns.astype(BF16).astype(F32)
    low = pltpu.roll(columns - high, LANES // 2, 1)
    return dot(jnp.where(iota(columns.shape, 1) < LANES // 2, high, low).astype(BF16), matrix)


def coupling(scal, deriv, other_l, other_c, t, w):
    drop = t * (scal[:, 0:1] - other_c[:, 0:1])
    columns = (t * w) * scal + (t * (1.0 - w)) * other_c
    return w * drop, ((1.0 - w) * drop) * other_l, columns


def local_kernel(count, nx, ny, wx, wy, c_ref, l_ref, a_ref, cell_ref, slot_ref, ft_ref, fu_ref, own_ref, base_ref, info_ref, pick_ref, put_ref, ls_ref):
    cells, width = l_ref.shape
    devices = nx * ny
    lane = lanes_of(count)
    scal = c_ref[...]
    ls_ref[...] = jnp.zeros_like(ls_ref)
    ls_ref[:, 0:width] = a_ref[...]
    accum = ls_ref[...]
    ls_ref[:, 0:width] = l_ref[...]
    deriv = ls_ref[...]
    at = iota((cells, 1), 0)
    at_x, at_y = at // wy, at & (wy - 1)
    first = spread_matrix(count)

    def col(value, name):
        return value[:, lane[name] : lane[name] + 1]

    scale = jnp.zeros((cells, 1), F32)
    total = jnp.zeros((cells, LANES), F32)
    steps = [(wy, "tx", "ux", at_x == 0), (cells - wy, "tx", "ux", at_x == wx - 1), (1, "ty", "uy", at_y == 0), (cells - 1, "ty", "uy", at_y == wy - 1)]
    for i, (step, trans, up, rim) in enumerate(steps):
        other_c, other_l = pltpu.roll(scal, step, 0), pltpu.roll(deriv, step, 0)
        if i % 2 == 0:
            t, w = col(other_c, trans), 1.0 - col(other_c, up)
        else:
            t, w = col(scal, trans), col(scal, up)
        t = jnp.where(rim, 0.0, t)
        share, moved, columns = coupling(scal, deriv, other_l, other_c, t, w)
        part = spread(columns, first)
        scale = scale + share
        total = total + part
        base_ref[(i + 1) * cells : (i + 2) * cells, :] = moved - part
    base_ref[0:cells, :] = accum + scale * deriv + total
    base_ref[5 * cells : 6 * cells, :] = deriv

    kcell = (iota((cells, cells), 0) == cell_ref[...]).astype(F32)
    info = jnp.concatenate(
        [slot_ref[...].astype(F32), ft_ref[...], fu_ref[...].astype(F32), jnp.zeros((5, cells), F32)], 0
    )
    info = dot(kcell, info, NT, EXACT)
    info_ref[...] = info
    slot = info[:, 0:1].astype(jnp.int32)
    place = first_order(slot >> 1, nx, ny) * GROUP + (slot & 1)
    pick_ref[...] = onehot(iota((cells, devices * GROUP), 1) == place)

    owner = own_ref[...]
    hits = (iota((devices, cells), 0) == owner).astype(F32)
    before = (iota((cells, cells), 0) < iota((cells, cells), 1)).astype(F32).astype(BF16)
    earlier = dot(hits.astype(BF16), before)
    rank = jnp.sum(earlier * hits, 0, keepdims=True)
    target = owner * GROUP + rank.astype(jnp.int32)
    put_ref[...] = onehot(iota((devices * GROUP, cells), 0) == target)


def rows_kernel(nx, ny, count, c_ref, base_ref, info_ref, pick_ref, put_ref, arr_ref, out_ref):
    cells = c_ref.shape[0]
    groups = arr_ref.shape[1] - 1
    side = groups * GROUP
    wx = wy = side
    devices = out_ref.shape[0]
    lane = lanes_of(count)
    width = count * count
    first = spread_matrix(count)

    def repeat(edge):
        return jnp.broadcast_to(edge[:, None, :], (wx, wy, LANES)).reshape(cells, LANES)

    def lows(deriv, name, spare):
        moved = pltpu.roll(deriv, LANES + lane[name] - (width + spare), 1)
        return jnp.where(iota(deriv.shape, 1) == lane[name], moved, 0.0)

    near = neighbours(nx, ny)
    there = [jnp.where(ok, 1.0, 0.0) for _, ok in near]
    edge_l = [jnp.where(ok, arr_ref[n, 0:groups].astype(F32).reshape(side, LANES), 0.0) for n, ok in near]
    tiles = [jnp.where(ok, arr_ref[n, groups].astype(F32), 0.0) for n, ok in near]
    packed = [jnp.broadcast_to(tile[row : row + 1], (8, LANES)) for tile in tiles for row in (2, 3)]
    packed = jnp.concatenate(packed, 0)
    packed = jnp.where(own_lanes(4 * side), packed, 0.0).astype(BF16)
    edge_c = []
    for i, name in ((0, "tx"), (2, "ty")):
        both = jnp.concatenate(edge_l[i : i + 2], 0)
        scal = dot(packed[i * side : (i + 2) * side], repeat_lanes(count, i), NT)
        edge_c.append(scal + lows(both, "p", 0) + lows(both, name, 1 if i == 0 else 2))
    edge_c = jnp.concatenate(edge_c, 0)

    tail = arr_ref[:, groups].astype(F32).reshape(devices * GROUP, LANES)
    tail = jnp.concatenate([tail.astype(BF16), pltpu.roll(tail, devices * GROUP - 2, 0).astype(BF16)], 1)
    far = dot(pick_ref[...], tail)
    far_l = far[:, 0:LANES]
    far_c = pltpu.roll(far[:, LANES:], LANES - 8 * SLOT, 1) + lows(far_l, "p", 0)

    edges = [pl.ds(0, wy), pl.ds(cells - wy, wy), pl.ds(0, wx, stride=wy), pl.ds(wy - 1, wx, stride=wy)]
    self_c = [c_ref[rows, :] for rows in edges]
    start = 5 * cells
    edges = [pl.ds(start, wy), pl.ds(start + cells - wy, wy), pl.ds(start, wx, stride=wy), pl.ds(start + wy - 1, wx, stride=wy)]
    self_l = jnp.concatenate([base_ref[rows, :] for rows in edges], 0)

    def col(value, name):
        return value[:, lane[name] : lane[name] + 1]

    t, w = [], []
    for i, (trans, up) in enumerate([("tx", "ux"), ("tx", "ux"), ("ty", "uy"), ("ty", "uy")]):
        other = edge_c[i * side : (i + 1) * side]
        t.append(col(other, trans) if i % 2 == 0 else col(self_c[i], trans) * there[i])
        w.append(1.0 - col(other, up) if i % 2 == 0 else col(self_c[i], up))
    t, w = jnp.concatenate(t, 0), jnp.concatenate(w, 0)
    share, moved, columns = coupling(jnp.concatenate(self_c, 0), self_l, jnp.concatenate(edge_l, 0), edge_c, t, w)
    part = spread(columns, first)
    off = moved - part
    add = share * self_l + part

    deriv = base_ref[start : start + cells, :]
    far_share, far_moved, far_columns = coupling(c_ref[...], deriv, far_l, far_c, info_ref[:, 1:2], info_ref[:, 2:3])
    far_part = spread(far_columns, first)

    at_y = iota((cells, 1), 0) & (wy - 1)
    low_y, high_y = at_y == 0, at_y == wy - 1

    def edge(value, i):
        return value[i * side : (i + 1) * side]

    def block(i):
        return base_ref[i * cells : (i + 1) * cells, :]

    diag = block(0) + far_share * deriv + far_part
    diag = diag + jnp.where(low_y, repeat(edge(add, 2)), 0.0) + jnp.where(high_y, repeat(edge(add, 3)), 0.0)
    diag = diag + jnp.concatenate([edge(add, 0), jnp.zeros((cells - 2 * wy, LANES), F32), edge(add, 1)], 0)
    xl, xh = block(1), block(2)
    xl = jnp.concatenate([xl[0:wy] + edge(off, 0), xl[wy:]], 0)
    xh = jnp.concatenate([xh[0 : cells - wy], xh[cells - wy :] + edge(off, 1)], 0)
    yl = jnp.where(low_y, repeat(edge(off, 2)), block(3))
    yh = jnp.where(high_y, repeat(edge(off, 3)), block(4))
    blocks = [value.astype(BF16) for value in (diag, xl, xh, yl, yh, far_moved - far_part)]
    for i in range(0, SENT, 2):
        pair = dot(put_ref[...], jnp.concatenate(blocks[i : i + 2], 1)).reshape(devices, GROUP, 2 * LANES)
        out_ref[:, i] = pair[:, :, 0:LANES].astype(BF16)
        out_ref[:, i + 1] = pair[:, :, LANES:].astype(BF16)


def expand_kernel(count, in_ref, out_ref, full_ref, sems):
    chunks = sems.shape[0]
    wide = out_ref.shape[2]
    group = 8
    tall, deep = group * 4 * BLOCKS, group * 4 * SENT
    o, i = iota((tall, deep), 0), iota((tall, deep), 1)
    block = o & 7
    want = (o >> 5) * (SENT * 4) + jnp.where(block == 7, 5, block) * 4 + ((o >> 3) & 3)
    order = ((block != 5) & (block != 6) & (i == want)).astype(F32).astype(BF16)
    src, to = iota((LANES, wide), 0), iota((LANES, wide), 1)
    r, c = to // PAD, to % PAD
    widen = ((r < count) & (c < count) & (src == r * count + c)).astype(F32).astype(BF16)
    groups = in_ref.shape[0] // deep
    per = tall // BLOCKS
    span = groups // chunks
    ordered = []

    def order_pair(g):
        pair = [in_ref[h * deep : (h + 1) * deep, :] for h in (g, g + 1)]
        rows = dot(order, jnp.concatenate(pair, 1)).astype(BF16)
        ordered.extend([rows[:, 0:LANES], rows[:, LANES:]])

    ahead = 2 * 4
    for g in range(0, ahead, 2):
        order_pair(g)
    copies = []
    for chunk in range(chunks):
        if len(ordered) < groups:
            order_pair(len(ordered))
        for g in range(chunk * span, (chunk + 1) * span):
            full = dot(ordered[g], widen)
            full_ref[g * per : (g + 1) * per] = full.reshape(per, BLOCKS, wide).astype(BF16)
        part = pl.ds(chunk * span * per, span * per)
        copy = pltpu.make_async_copy(full_ref.at[part], out_ref.at[part], sems.at[chunk])
        copy.start()
        copies.append(copy)
    for copy in copies:
        copy.wait()


def body(pressure, mobility, mob_deriv, accum, trans, upwind, fault_send, fault_cell, fault_slot, fault_trans, fault_up, cell_owner):
    wx, wy, _ = pressure.shape
    count = mobility.shape[0]
    cells = wx * wy
    nx, ny = lax.axis_size("tx"), lax.axis_size("ty")
    devices = nx * ny
    deriv = jnp.transpose(mob_deriv, (1, 2, 3, 0)).reshape(cells, count * count)
    accumulated = jnp.transpose(accum, (1, 2, 3, 0)).reshape(cells, count * count)
    side = max(wx, wy)
    packed = (fault_send[0].T, pressure[..., 0], mobility[..., 0], trans[..., 0], upwind[..., 0], deriv)
    scal, outgoing = pl.pallas_call(
        functools.partial(pack_kernel, nx, ny),
        out_shape=(
            jax.ShapeDtypeStruct((cells, LANES), F32),
            jax.ShapeDtypeStruct((devices, side // GROUP + 1, GROUP, LANES), BF16),
        ),
        in_specs=[pl.BlockSpec(memory_space=pl.ANY)] * len(packed),
        out_specs=[pl.BlockSpec(memory_space=pl.ANY)] * 2,
        scratch_shapes=[
            *[pltpu.VMEM(value.shape, value.dtype) for value in packed],
            pltpu.VMEM((cells, LANES), F32),
            pltpu.VMEM((cells, LANES), F32),
            pltpu.VMEM((cells, LANES), F32),
            pltpu.VMEM((devices, GROUP, LANES), BF16),
            pltpu.VMEM((4, side // GROUP, GROUP, LANES), BF16),
            pltpu.VMEM((devices * GROUP, cells), BF16),
            pltpu.SemaphoreType.DMA((6,)),
            pltpu.SemaphoreType.DMA((len(packed),)),
        ],
        name="pack",
    )(*packed)
    arrived = lax.all_to_all(outgoing, ("ty", "tx"), split_axis=0, concat_axis=0, tiled=True)
    base, info, pick, put = pl.pallas_call(
        functools.partial(local_kernel, count, nx, ny, wx, wy),
        out_shape=(
            jax.ShapeDtypeStruct((6 * cells, LANES), F32),
            jax.ShapeDtypeStruct((cells, 8), F32),
            jax.ShapeDtypeStruct((cells, devices * GROUP), BF16),
            jax.ShapeDtypeStruct((devices * GROUP, cells), BF16),
        ),
        scratch_shapes=[pltpu.VMEM((cells, LANES), F32)],
        compiler_params=pltpu.CompilerParams(vmem_limit_bytes=12 << 20),
        cost_estimate=pl.CostEstimate(flops=2 << 27, bytes_accessed=8 << 20, transcendentals=0),
        name="local",
    )(
        scal, deriv, accumulated,
        fault_cell, fault_slot, fault_trans, fault_up, cell_owner.reshape(1, cells),
    )
    buffer = pl.pallas_call(
        functools.partial(rows_kernel, nx, ny, count),
        out_shape=jax.ShapeDtypeStruct((devices, SENT, GROUP, LANES), BF16),
        compiler_params=pltpu.CompilerParams(vmem_limit_bytes=16 << 20),
        name="rows",
    )(scal, base, info, pick, put, arrived)
    landed = lax.all_to_all(buffer, ("tx", "ty"), split_axis=0, concat_axis=0, tiled=True)
    landed = landed.reshape(devices * SENT * 4, LANES)
    relaid = jax.ShapeDtypeStruct((devices * 4, BLOCKS, PAD * PAD), BF16)
    chunks = 8
    return pl.pallas_call(
        functools.partial(expand_kernel, count),
        out_shape=relaid,
        out_specs=pl.BlockSpec(memory_space=pl.ANY),
        scratch_shapes=[pltpu.VMEM(relaid.shape, BF16), pltpu.SemaphoreType.DMA((chunks,))],
        compiler_params=pltpu.CompilerParams(vmem_limit_bytes=16 << 20),
        name="expand",
    )(landed)


def solution(mesh):
    in_specs = (
        P("tx", "ty", None),
        P(None, "tx", "ty", None),
        P(None, "tx", "ty", None),
        P(None, "tx", "ty", None),
        P(None, "tx", "ty", None),
        P(None, "tx", "ty", None),
        P(("tx", "ty"), None, None),
        P(("tx", "ty"), None),
        P(("tx", "ty"), None),
        P(("tx", "ty"), None),
        P(("tx", "ty"), None),
        P(("tx", "ty"), None),
    )
    out_specs = P(("tx", "ty"), None, None)
    return jax.shard_map(body, mesh=mesh, in_specs=in_specs, out_specs=out_specs, check_vma=False)
```
